128 devices in a mesh: outer: 16 (over z, x_lo, core), inner: 8 (over y, x_hi).
Axes of the slice: x: 4 (x_hi: 2, x_lo: 2; x = x_hi * 2 + x_lo), y: 4, z: 4, core: 2. Of those that a mesh axis runs over, the one named last changes fastest.
Arguments:
- queries: bfloat16 [8, 16384, 128], P(None, ('outer', 'inner')), may hold values from -6 to 6
- key_states: bfloat16 [16384, 128], P(('outer', 'inner')), may hold values from -6 to 6
- value_states: bfloat16 [16384, 128], P(('outer', 'inner')), may hold values from -6 to 6
- outputs: bfloat16 [8, 16384, 128], P(None, ('outer', 'inner')), may hold values from -6 to 6
- grad_outputs: bfloat16 [8, 16384, 128], P(None, ('outer', 'inner')), may hold values from -6 to 6
- log_sums: float32 [8, 16384], P(None, ('outer', 'inner')), may hold values from -1 to 20
- span_order: int32 [256], replicated, may hold values from 0 to 255, as said below
Outputs:
- query_grads: bfloat16 [8, 16384, 128], P(None, ('outer', 'inner'))
- key_grads: bfloat16 [16384, 128], P(('outer', 'inner'))
- value_grads: bfloat16 [16384, 128], P(('outer', 'inner'))
The draws below stay inside these ranges and needn't reach their ends.
Inputs may be any that keep to these rules, and one draw needn't show every extreme that they name: span_order is a permutation of the 256 position blocks; entries 2 d and 2 d + 1 (the blocks stored on device d) add up to 255.
All inputs are finite; a program needn't handle non-finite values.
Results may differ from the reference program's by a relative error of at most 0.0052.
Values may be sent and summed in bfloat16 or wider, within the bound.
No kernel may reach another device: no remote copies, remote signals or barrier semaphores. Data moves between devices by JAX's collectives and lax.ppermute only.
A program may use at most 64 MiB of HBM per device.

```python
import math
import jax
import jax.numpy as jnp
from jax import lax

DH = 128
H = 8
SPAN = 64
BLOCKS = 256
TOKENS = 16384


def block_order(key):
    order_key = jax.random.fold_in(key, 11)
    half_blocks = BLOCKS // 2
    chosen = jax.random.permutation(jax.random.fold_in(order_key, 1), half_blocks).astype(jnp.int32)
    flips = jax.random.randint(jax.random.fold_in(order_key, 2), (half_blocks,), 0, 2).astype(jnp.int32)
    first_block = jnp.where(flips == 1, BLOCKS - 1 - chosen, chosen)
    second_block = BLOCKS - 1 - first_block
    return jnp.stack([first_block, second_block], axis=1).reshape(BLOCKS).astype(jnp.int32)


def draw_span_order(key, part):
    return block_order(key)


def draw_log_sums(key, part):
    order = block_order(key)
    row_ids = jnp.arange(TOKENS, dtype=jnp.int32)
    seq_pos = order[row_ids // SPAN] * SPAN + row_ids % SPAN
    baseline = jnp.log(seq_pos.astype(jnp.float32) + 1.0)
    noise_key = jax.random.fold_in(key, 23)
    offsets = jax.random.uniform(noise_key, (H, TOKENS), jnp.float32, 0.2, 0.8)
    return baseline[None, :] + offsets


def levels(key, extent, shards, smallest, largest):
    def one(dim, blocks):
        heights = jax.random.uniform(jax.random.fold_in(jax.random.fold_in(key, 6), dim), (blocks,), jnp.float32, smallest / len(shards), largest / len(shards))
        return jnp.repeat(jnp.exp(heights), extent[dim] // blocks).reshape((-1,) + (1,) * (len(extent) - dim - 1))

    loudness = one(*shards[0])
    for cut in shards[1:]:
        loudness = loudness * one(*cut)
    return loudness


def noise(stream_key, extent, spread, reach, cuts=(), held_as=jnp.bfloat16):
    gain = levels(stream_key, extent, cuts, -0.22, 0.18) if cuts else 1.0
    result = jax.random.normal(stream_key, extent, jnp.float32) * spread * gain
    return jnp.minimum(jnp.maximum(result, -reach), reach).astype(held_as)


def setup_inputs(seed: int = 0) -> dict:
    seeds = jax.random.split(jax.random.key(seed), 8)
    queries = noise(seeds[0], (H, TOKENS, DH), 1.0, 6.0, ((1, 128),))
    key_states = noise(seeds[1], (TOKENS, DH), 1.0, 6.0, ((0, 128),))
    value_states = noise(seeds[2], (TOKENS, DH), 1.0, 6.0, ((0, 128),))
    outputs = noise(seeds[3], (H, TOKENS, DH), 1.0, 6.0, ((1, 128),))
    grad_outputs = noise(seeds[4], (H, TOKENS, DH), 1.0, 6.0, ((1, 128),))
    log_sums = draw_log_sums(jax.random.fold_in(seeds[7], 71), 0)
    span_order = draw_span_order(jax.random.fold_in(seeds[7], 71), 0)
    return {"queries": queries, "key_states": key_states, "value_states": value_states, "outputs": outputs, "grad_outputs": grad_outputs, "log_sums": log_sums, "span_order": span_order}


def positions(span_order):
    row_ids = jnp.arange(TOKENS, dtype=jnp.int32)
    return (span_order[row_ids // SPAN] * SPAN + row_ids % SPAN).astype(jnp.int32)

def reference(queries, key_states, value_states, outputs, grad_outputs, log_sums, span_order):
    softmax_scale = 1.0 / math.sqrt(DH)
    seq_pos = positions(span_order)
    deltas = lax.optimization_barrier(jnp.sum(grad_outputs.astype(jnp.float32) * outputs.astype(jnp.float32), axis=-1))
    query_block = math.gcd(256, TOKENS)
    block_count = TOKENS // query_block

    def one_block(carried, block_index):
        grad_keys, grad_values = carried
        first_row = (block_index * query_block).astype(jnp.int32)
        query_rows = lax.dynamic_slice_in_dim(queries, first_row, query_block, 1).reshape(H * query_block, DH)
        grad_rows = lax.dynamic_slice_in_dim(grad_outputs, first_row, query_block, 1).reshape(H * query_block, DH)
        log_norm = lax.dynamic_slice_in_dim(log_sums, first_row, query_block, 1).reshape(H * query_block, 1)
        delta_rows = lax.dynamic_slice_in_dim(deltas, first_row, query_block, 1).reshape(H * query_block, 1)
        query_pos = jnp.tile(lax.dynamic_slice_in_dim(seq_pos, first_row, query_block, 0), H)
        scores = jnp.dot(query_rows, key_states.T, preferred_element_type=jnp.float32) * softmax_scale
        visible = query_pos[:, None] >= seq_pos[None, :]
        attend = jnp.where(visible, jnp.exp(scores - log_norm), jnp.float32(0.0))
        grad_prob = jnp.dot(grad_rows, value_states.T, preferred_element_type=jnp.float32)
        grad_score = attend * (grad_prob - delta_rows)
        attend_low = attend.astype(jnp.bfloat16)
        score_low = grad_score.astype(jnp.bfloat16)
        grad_values = grad_values + jnp.dot(attend_low.T, grad_rows, preferred_element_type=jnp.float32)
        grad_keys = grad_keys + jnp.dot(score_low.T, query_rows, preferred_element_type=jnp.float32) * softmax_scale
        grad_query = jnp.dot(score_low, key_states, preferred_element_type=jnp.float32) * softmax_scale
        return ((grad_keys, grad_values), grad_query.astype(jnp.bfloat16).reshape(H, query_block, DH))
    initial = (jnp.zeros((TOKENS, DH), jnp.float32), jnp.zeros((TOKENS, DH), jnp.float32))
    (grad_keys, grad_values), pieces = lax.scan(one_block, initial, jnp.arange(block_count, dtype=jnp.int32))
    query_grads = jnp.transpose(pieces, (1, 0, 2, 3)).reshape(H, TOKENS, DH)
    return (query_grads, grad_keys.astype(jnp.bfloat16), grad_values.astype(jnp.bfloat16))
```

```python
import functools
import math

import jax
import jax.numpy as jnp
from jax import lax
from jax.experimental import pallas as pl
from jax.experimental.pallas import tpu as pltpu
from jax.sharding import Mesh
from jax.sharding import PartitionSpec as P

f32 = jnp.float32
bf16 = jnp.bfloat16
NT = (((1,), (1,)), ((), ()))
NN = (((1,), (0,)), ((), ()))
LOG2E = 1.0 / math.log(2.0)
AXES = ("z", "xl", "c", "y", "xh")
SIZES = (4, 2, 2, 4, 2)
WIDE = 4


def dot(a, b, dims):
    return lax.dot_general(a, b, dims, preferred_element_type=f32)


def kernel(
    first, scale, order, sorted_pos, query_block, below, own,
    qd_ref, st_ref, kv_ref, *rest,
):
    if first:
        dq_ref, dkv_ref, ks, vs, kt, dk, dv, dq = rest
    else:
        prev_ref, dq_ref, dkv_ref, ks, vs, kt, dk, dv, dq = rest
    groups, rows = qd_ref.shape[0], qd_ref.shape[2]
    blocks, span, _ = kv_ref.shape
    width = qd_ref.shape[3]
    chunk = WIDE * span
    for r in range(blocks):
        block = kv_ref[order[r]]
        ks[r * span : (r + 1) * span, :] = block[:, :width]
        vs[r * span : (r + 1) * span, :] = block[:, width:]
        if first:
            dk[r * span : (r + 1) * span, :] = jnp.zeros((span, width), f32)
            dv[r * span : (r + 1) * span, :] = jnp.zeros((span, width), f32)
        else:
            part = prev_ref[order[r]]
            dk[r * span : (r + 1) * span, :] = part[:, :width]
            dv[r * span : (r + 1) * span, :] = part[:, width:]
    for r in range(0, blocks * span, chunk):
        kt[:, r : r + chunk] = ks[r : r + chunk, :].T

    def unit(g, i, masked):
        at = pl.ds(pl.multiple_of(i * chunk, chunk), chunk)
        q, do = qd_ref[g, 0], qd_ref[g, 1]
        k, v = ks[at, :], vs[at, :]
        s = dot(k, q, NT)
        p = jnp.exp2(s * (scale * LOG2E) - st_ref[g, 0:1, :])
        if masked:
            lead = lax.rem(lax.broadcasted_iota(jnp.int32, (span, rows), 1), span)
            lead = lead - lax.broadcasted_iota(jnp.int32, (span, rows), 0)
            seen = [
                lead + (query_block[g] - sorted_pos[i * WIDE + j]) * span for j in range(WIDE)
            ]
            p = jnp.where(jnp.concatenate(seen, axis=0) >= 0, p, 0.0)
        dp = dot(v, do, NT)
        ds = (p * (dp - st_ref[g, 1:2, :])).astype(bf16)
        dv[at, :] += dot(p.astype(bf16), do, NN)
        dk[at, :] += dot(ds, q, NN)
        dq[...] += dot(kt[:, at], ds, NN)

    def group(g, carry):
        dq[...] = jnp.zeros_like(dq)
        whole = below[g] // WIDE

        def step(i, carry):
            unit(g, i, False)
            return carry

        lax.fori_loop(0, whole, step, 0)

        @pl.when(whole * WIDE < below[g] + own[g])
        def _():
            unit(g, whole, True)

        for j in range(0, rows, width):
            dq_ref[g, j : j + width, :] = dq[:, j : j + width].T.astype(dq_ref.dtype)
        return carry

    lax.fori_loop(0, groups, group, 0)
    for r in range(blocks):
        at = pl.ds(r * span, span)
        dkv_ref[order[r]] = jnp.concatenate([dk[at, :], dv[at, :]], axis=1).astype(dkv_ref.dtype)


def attend(tables, qd, st, kv, prev, dq_type, dkv_type, name):
    groups, _, rows, width = qd.shape
    blocks, span, _ = kv.shape
    vmem = pl.BlockSpec(memory_space=pltpu.VMEM)
    smem = pl.BlockSpec(memory_space=pltpu.SMEM)
    args = (qd, st, kv) + (() if prev is None else (prev,))
    scale = 1.0 / math.sqrt(width)
    pairs = groups * rows * blocks * span // 2
    return pl.pallas_call(
        functools.partial(kernel, prev is None, scale),
        out_shape=(
            jax.ShapeDtypeStruct((groups, rows, width), dq_type),
            jax.ShapeDtypeStruct(kv.shape, dkv_type),
        ),
        in_specs=[smem] * len(tables) + [vmem] * len(args),
        out_specs=(vmem, vmem),
        scratch_shapes=[
            pltpu.VMEM((blocks * span, width), bf16),
            pltpu.VMEM((blocks * span, width), bf16),
            pltpu.VMEM((width, blocks * span), bf16),
            pltpu.VMEM((blocks * span, width), f32),
            pltpu.VMEM((blocks * span, width), f32),
            pltpu.VMEM((width, rows), f32),
        ],
        cost_estimate=pl.CostEstimate(
            flops=pairs * width * 20, transcendentals=pairs, bytes_accessed=8 << 20
        ),
        compiler_params=pltpu.CompilerParams(vmem_limit_bytes=40 << 20),
        name=name,
    )(*tables, *args)


def lookup(table, ids):
    hits = ids[:, None] == jnp.arange(table.shape[0], dtype=jnp.int32)[None, :]
    return jnp.sum(jnp.where(hits, table[None, :], 0), axis=1)


def rank(z, xl, c, y, xh):
    return (((z * 2 + xl) * 2 + c) * 4 + y) * 2 + xh


def body(q, k, v, o, do, log_sums, span_order):
    heads, tokens, width = q.shape
    span = tokens // 2
    rows = heads * span
    scale = 1.0 / math.sqrt(width)
    z, xl, c, y, xh = [lax.axis_index(a) for a in AXES]

    kv = jnp.concatenate([k, v], axis=1)
    kv = lax.all_to_all(
        jnp.broadcast_to(kv[None], (16, tokens, 2 * width)), ("z", "y"), 0, 0, tiled=True
    ).reshape(32, span, 2 * width)

    def split(a):
        return a.reshape(heads, 2, span, width).transpose(1, 0, 2, 3).reshape(2, rows, width)

    qd = jnp.stack([split(q), split(do)], axis=1)
    delta = jnp.sum(do.astype(f32) * o.astype(f32), axis=-1)
    st = jnp.stack([log_sums * LOG2E, delta]).reshape(2, heads, 2, span)
    st = st.transpose(2, 0, 1, 3).reshape(2, 2, rows)
    qd = lax.all_to_all(
        jnp.broadcast_to(qd[None], (4, *qd.shape)), ("xl", "xh"), 0, 0, tiled=True
    ).reshape(8, 2, rows, width)
    st = lax.all_to_all(
        jnp.broadcast_to(st[None], (4, *st.shape)), ("xl", "xh"), 0, 0, tiled=True
    ).reshape(8, 2, rows)
    swap = [(0, 1), (1, 0)]
    qd_far = lax.ppermute(qd, "c", swap)
    st_far = lax.ppermute(st, "c", swap)

    i4 = jnp.arange(4, dtype=jnp.int32)
    i16 = jnp.arange(16, dtype=jnp.int32)
    kv_ids = rank(i16 // 4, xl, c, i16 % 4, xh)
    q_ids = jnp.concatenate([rank(z, i4 // 2, cc, y, i4 % 2) for cc in (c, 1 - c)])
    ids = jnp.concatenate([kv_ids, q_ids])
    ids = (ids[:, None] * 2 + jnp.arange(2, dtype=jnp.int32)[None, :]).reshape(48)
    pos = lookup(span_order, ids)
    kv_pos, q_pos = pos[:32], pos[32:]
    place = jnp.sum((kv_pos[None, :] < kv_pos[:, None]).astype(jnp.int32), axis=1)
    hit = place[:, None] == jnp.arange(32, dtype=jnp.int32)[None, :]
    order = jnp.sum(jnp.where(hit, jnp.arange(32, dtype=jnp.int32)[:, None], 0), axis=0)
    sorted_pos = jnp.sum(jnp.where(hit, kv_pos[:, None], 0), axis=0)
    below = jnp.sum((kv_pos[None, :] < q_pos[:, None]).astype(jnp.int32), axis=1)
    own = jnp.sum((kv_pos[None, :] == q_pos[:, None]).astype(jnp.int32), axis=1)

    near = (order, sorted_pos, q_pos[:8], below[:8], own[:8])
    far = (order, sorted_pos, q_pos[8:], below[8:], own[8:])
    dq_near, dkv = attend(near, qd, st, kv, None, f32, f32, "near")
    dq_far, dkv = attend(far, qd_far, st_far, kv, dkv, f32, bf16, "far")

    dkv = lax.all_to_all(dkv.reshape(16, tokens, 2 * width), ("z", "y"), 0, 0, tiled=True)
    dkv = jnp.sum(dkv.astype(f32), axis=0)
    dk = (dkv[:, :width] * scale).astype(bf16)
    dv = dkv[:, width:].astype(bf16)

    dq = (dq_near + lax.ppermute(dq_far, "c", swap)).astype(bf16)
    dq = lax.all_to_all(dq.reshape(4, 2, rows, width), ("xl", "xh"), 0, 0, tiled=True)
    dq = jnp.sum(dq.astype(f32), axis=0) * scale
    dq = dq.reshape(2, heads, span, width).transpose(1, 0, 2, 3).reshape(heads, tokens, width)
    return dq.astype(bf16), dk, dv


def solution(mesh):
    fine = Mesh(mesh.devices.reshape(SIZES), AXES)
    return jax.shard_map(
        body,
        mesh=fine,
        in_specs=(
            P(None, AXES, None),
            P(AXES, None),
            P(AXES, None),
            P(None, AXES, None),
            P(None, AXES, None),
            P(None, AXES),
            P(),
        ),
        out_specs=(P(None, AXES, None), P(AXES, None), P(AXES, None)),
        check_vma=False,
    )
```

```python
import functools
import math

import jax
import jax.numpy as jnp
from jax import lax
from jax.experimental import pallas as pl
from jax.experimental.pallas import tpu as pltpu
from jax.sharding import Mesh
from jax.sharding import PartitionSpec as P

f32 = jnp.float32
bf16 = jnp.bfloat16
NT = (((1,), (1,)), ((), ()))
NN = (((1,), (0,)), ((), ()))
LOG2E = 1.0 / math.log(2.0)
AXES = ("z", "xl", "c", "y", "xh")
SIZES = (4, 2, 2, 4, 2)
WIDE = 4
UNROLL = 2
STAT_ROWS = 32


def dot(a, b, dims):
    return lax.dot_general(a, b, dims, preferred_element_type=f32)


def kernel(
    counts, scale, order, sorted_pos, query_block, below, own, kv_ref, *rest
):
    payloads, rest = rest[: len(counts)], rest[len(counts) :]
    dq_ref, dkv_ref, qs, dos, st, ks, vs, kt, dk, dv, dq = rest
    groups, rows, width = qs.shape
    blocks, span, _ = kv_ref.shape
    chunk = WIDE * span
    for r in range(blocks):
        block = kv_ref[order[r]]
        ks[r * span : (r + 1) * span, :] = block[:, :width]
        vs[r * span : (r + 1) * span, :] = block[:, width:]
    dk[...] = jnp.zeros_like(dk)
    dv[...] = jnp.zeros_like(dv)
    for r in range(0, blocks * span, chunk):
        kt[:, r : r + chunk] = ks[r : r + chunk, :].T
    g = 0
    lines = rows // width
    for ref, count in zip(payloads, counts):
        for i in range(count):
            qs[g] = ref[i, :rows, :]
            dos[g] = ref[i, rows : 2 * rows, :]
            terms = ref[i, 2 * rows :, :].astype(f32)
            for kind in range(2):
                t = terms[kind * 3 * lines :]
                t = t[:lines] + t[lines : 2 * lines] + t[2 * lines : 3 * lines]
                st[g, kind : kind + 1, :] = jnp.concatenate(
                    [t[j : j + 1] for j in range(lines)], axis=1
                )
            g += 1

    def unit(g, first, count, masked):
        q, do = qs[g], dos[g]
        log_norm, delta = st[g, 0:1, :], st[g, 1:2, :]
        total = None
        for n in range(count):
            at = pl.ds(pl.multiple_of((first + n) * chunk, chunk), chunk)
            k, v = ks[at, :], vs[at, :]
            s = dot(k, q, NT)
            dp = dot(v, do, NT)
            p = jnp.exp2(s * (scale * LOG2E) - log_norm)
            if masked:
                lead = lax.rem(lax.broadcasted_iota(jnp.int32, (span, rows), 1), span)
                lead = lead - lax.broadcasted_iota(jnp.int32, (span, rows), 0)
                seen = [
                    lead + (query_block[g] - sorted_pos[(first + n) * WIDE + j]) * span
                    for j in range(WIDE)
                ]
                p = jnp.where(jnp.concatenate(seen, axis=0) >= 0, p, 0.0)
            ds = (p * (dp - delta)).astype(bf16)
            dv[at, :] += dot(p.astype(bf16), do, NN)
            dk[at, :] += dot(ds, q, NN)
            part = dot(kt[:, at], ds, NN)
            total = part if total is None else total + part
        dq[...] += total

    def group(g, carry):
        dq[...] = jnp.zeros_like(dq)
        whole = below[g] // WIDE
        pairs = whole // UNROLL

        def step(i, carry):
            unit(g, i * UNROLL, UNROLL, False)
            return carry

        def single(i, carry):
            unit(g, i, 1, False)
            return carry

        lax.fori_loop(0, pairs, step, 0)
        lax.fori_loop(pairs * UNROLL, whole, single, 0)

        @pl.when(whole * WIDE < below[g] + own[g])
        def _():
            unit(g, whole, 1, True)

        for j in range(0, rows, width):
            dq_ref[g, j : j + width, :] = dq[:, j : j + width].T.astype(dq_ref.dtype)
        return carry

    lax.fori_loop(0, groups, group, 0)
    for r in range(blocks):
        at = pl.ds(r * span, span)
        dkv_ref[order[r]] = jnp.concatenate([dk[at, :], dv[at, :]], axis=1).astype(dkv_ref.dtype)


def attend(tables, kv, payloads, dq_type, dkv_type):
    counts = tuple(p.shape[0] for p in payloads)
    groups = sum(counts)
    rows = (payloads[0].shape[1] - STAT_ROWS) // 2
    blocks, span, width = kv.shape
    width = width // 2
    vmem = pl.BlockSpec(memory_space=pltpu.VMEM)
    smem = pl.BlockSpec(memory_space=pltpu.SMEM)
    args = (kv, *payloads)
    scale = 1.0 / math.sqrt(width)
    pairs = groups * rows * blocks * span // 2
    return pl.pallas_call(
        functools.partial(kernel, counts, scale),
        out_shape=(
            jax.ShapeDtypeStruct((groups, rows, width), dq_type),
            jax.ShapeDtypeStruct(kv.shape, dkv_type),
        ),
        in_specs=[smem] * len(tables) + [vmem] * len(args),
        out_specs=(vmem, vmem),
        scratch_shapes=[
            pltpu.VMEM((groups, rows, width), bf16),
            pltpu.VMEM((groups, rows, width), bf16),
            pltpu.VMEM((groups, 2, rows), f32),
            pltpu.VMEM((blocks * span, width), bf16),
            pltpu.VMEM((blocks * span, width), bf16),
            pltpu.VMEM((width, blocks * span), bf16),
            pltpu.VMEM((blocks * span, width), f32),
            pltpu.VMEM((blocks * span, width), f32),
            pltpu.VMEM((width, rows), f32),
        ],
        cost_estimate=pl.CostEstimate(
            flops=pairs * width * 20, transcendentals=pairs, bytes_accessed=8 << 20
        ),
        compiler_params=pltpu.CompilerParams(vmem_limit_bytes=40 << 20),
        name="attend",
    )(*tables, *args)


def lookup(table, ids):
    hits = ids[:, None] == jnp.arange(table.shape[0], dtype=jnp.int32)[None, :]
    return jnp.sum(jnp.where(hits, table[None, :], 0), axis=1)


def rank(z, xl, c, y, xh):
    return (((z * 2 + xl) * 2 + c) * 4 + y) * 2 + xh


def three_terms(x):
    high = lax.reduce_precision(x, 8, 7)
    middle = lax.reduce_precision(x - high, 8, 7)
    low = lax.reduce_precision(x - high - middle, 8, 7)
    return jnp.stack([high, middle, low])


def x_shift(a, by):
    at = lambda x: (x % 2) * 2 + x // 2
    return lax.ppermute(a, ("xl", "xh"), [(at(x), at((x + by) % 4)) for x in range(4)])


def swap(a):
    return lax.ppermute(a, "c", [(0, 1), (1, 0)])


def body(q, k, v, o, do, log_sums, span_order):
    heads, tokens, width = q.shape
    span = tokens // 2
    rows = heads * span
    scale = 1.0 / math.sqrt(width)
    z, xl, c, y, xh = [lax.axis_index(a) for a in AXES]
    x = xh * 2 + xl

    kv = jnp.concatenate([k, v], axis=1)
    kv = lax.all_to_all(
        jnp.broadcast_to(kv[None], (16, tokens, 2 * width)), ("z", "y"), 0, 0, tiled=True
    ).reshape(32, span, 2 * width)

    def split(a):
        return a.reshape(heads, 2, span, width).transpose(1, 0, 2, 3).reshape(2, rows, width)

    delta = jnp.sum(do.astype(f32) * o.astype(f32), axis=-1)
    st = jnp.stack([three_terms(log_sums * LOG2E), three_terms(delta)])
    st = st.reshape(6, heads, 2, span).transpose(2, 0, 1, 3).reshape(2, 6 * rows // width, width)
    st = jnp.pad(st, ((0, 0), (0, STAT_ROWS - st.shape[1]), (0, 0)))
    mine = jnp.concatenate([split(q), split(do), st.astype(bf16)], axis=1)
    right = x_shift(mine, 1)
    left = x_shift(mine, -1)
    across = (x_shift(right[:1], 1), x_shift(left[1:], -1))
    near = (mine, right, left, *across)
    far = tuple(swap(a) for a in near)

    i16 = jnp.arange(16, dtype=jnp.int32)
    kv_ids = rank(i16 // 4, xl, c, i16 % 4, xh)
    q_ids = []
    for cc in (c, 1 - c):
        for shift in (0, 3, 1, 2):
            xx = lax.rem(x + shift, 4)
            q_ids.append(rank(z, lax.rem(xx, 2), cc, y, xx // 2))
    ids = jnp.concatenate([kv_ids, jnp.stack(q_ids)])
    ids = (ids[:, None] * 2 + jnp.arange(2, dtype=jnp.int32)[None, :]).reshape(48)
    pos = lookup(span_order, ids)
    kv_pos, q_pos = pos[:32], pos[32:]
    place = jnp.sum((kv_pos[None, :] < kv_pos[:, None]).astype(jnp.int32), axis=1)
    hit = place[:, None] == jnp.arange(32, dtype=jnp.int32)[None, :]
    order = jnp.sum(jnp.where(hit, jnp.arange(32, dtype=jnp.int32)[:, None], 0), axis=0)
    sorted_pos = jnp.sum(jnp.where(hit, kv_pos[:, None], 0), axis=0)
    below = jnp.sum((kv_pos[None, :] < q_pos[:, None]).astype(jnp.int32), axis=1)
    own = jnp.sum((kv_pos[None, :] == q_pos[:, None]).astype(jnp.int32), axis=1)

    tables = (order, sorted_pos, q_pos, below, own)
    dq, dkv = attend(tables, kv, near + far, f32, bf16)

    dkv = lax.all_to_all(dkv.reshape(16, tokens, 2 * width), ("z", "y"), 0, 0, tiled=True)
    dkv = jnp.sum(dkv.astype(f32), axis=0)
    dk = (dkv[:, :width] * scale).astype(bf16)
    dv = dkv[:, width:].astype(bf16)

    dq = dq[:8] + swap(dq[8:])
    by_left = x_shift(dq[6:7].astype(bf16), -1)
    by_right = x_shift(dq[7:8].astype(bf16), 1)
    to_left = jnp.concatenate([dq[2:3] + by_left.astype(f32), dq[3:4]], axis=0)
    to_right = jnp.concatenate([dq[4:5], dq[5:6] + by_right.astype(f32)], axis=0)
    from_right = x_shift(to_left.astype(bf16), -1)
    from_left = x_shift(to_right.astype(bf16), 1)
    dq = (dq[:2] + from_right.astype(f32) + from_left.astype(f32)) * scale
    dq = dq.reshape(2, heads, span, width).transpose(1, 0, 2, 3).reshape(heads, tokens, width)
    return dq.astype(bf16), dk, dv


def solution(mesh):
    fine = Mesh(mesh.devices.reshape(SIZES), AXES)
    return jax.shard_map(
        body,
        mesh=fine,
        in_specs=(
            P(None, AXES, None),
            P(AXES, None),
            P(AXES, None),
            P(None, AXES, None),
            P(None, AXES, None),
            P(None, AXES),
            P(),
        ),
        out_specs=(P(None, AXES, None), P(AXES, None), P(AXES, None)),
        check_vma=False,
    )
```

```python
import functools
import math

import jax
import jax.numpy as jnp
from jax import lax
from jax.experimental import pallas as pl
from jax.experimental.pallas import tpu as pltpu
from jax.sharding import Mesh
from jax.sharding import PartitionSpec as P

f32 = jnp.float32
bf16 = jnp.bfloat16
NT = (((1,), (1,)), ((), ()))
NN = (((1,), (0,)), ((), ()))
LOG2E = 1.0 / math.log(2.0)
AXES = ("zh", "zl", "xl", "c", "yh", "yl", "xh")
KV_AXES = ("zh", "yl", "zl", "yh")
WIDE = 4
UNROLL = 2
STAT_ROWS = 32


def dot(a, b, dims):
    return lax.dot_general(a, b, dims, preferred_element_type=f32)


def kernel(
    counts, scale, order, sorted_pos, query_block, below, own, kv_ref, *rest
):
    payloads, rest = rest[: len(counts)], rest[len(counts) :]
    near_ref, far_ref, dkv_ref, qd, st, ks, vs, kt, dk, dv, dq, sems = rest
    groups, _, width = qd.shape
    rows = st.shape[2]
    copies, g = [], 0
    for n, (ref, count) in enumerate(zip(payloads, counts)):
        copies.append(pltpu.make_async_copy(ref, qd.at[pl.ds(g, count)], sems.at[n]))
        copies[-1].start()
        g += count
    blocks, span, _ = kv_ref.shape
    chunk = WIDE * span
    for r in range(blocks):
        block = kv_ref[order[r]]
        ks[r * span : (r + 1) * span, :] = block[:, :width]
        vs[r * span : (r + 1) * span, :] = block[:, width:]
    dk[...] = jnp.zeros_like(dk)
    dv[...] = jnp.zeros_like(dv)
    for r in range(0, blocks * span, chunk):
        kt[:, r : r + chunk] = ks[r : r + chunk, :].T
    lines = rows // width
    for copy in copies:
        copy.wait()
    for g in range(groups):
        terms = qd[g, 2 * rows :, :].astype(f32)
        for kind in range(2):
            t = terms[kind * 3 * lines :]
            t = t[:lines] + t[lines : 2 * lines] + t[2 * lines : 3 * lines]
            st[g, kind : kind + 1, :] = jnp.concatenate(
                [t[j : j + 1] for j in range(lines)], axis=1
            )

    def unit(g, first, count, size, masked):
        q, do = qd[g, :rows, :], qd[g, rows : 2 * rows, :]
        log_norm, delta = st[g, 0:1, :], st[g, 1:2, :]
        total = None
        for n in range(count):
            at = pl.ds(pl.multiple_of((first + n) * chunk, chunk), size * span)
            k, v = ks[at, :], vs[at, :]
            s = dot(k, q, NT)
            dp = dot(v, do, NT)
            p = jnp.exp2(s * (scale * LOG2E) - log_norm)
            if masked:
                lead = lax.rem(lax.broadcasted_iota(jnp.int32, (span, rows), 1), span)
                lead = lead - lax.broadcasted_iota(jnp.int32, (span, rows), 0)
                seen = [
                    lead + (query_block[g] - sorted_pos[(first + n) * WIDE + j]) * span
                    for j in range(size)
                ]
                p = jnp.where(jnp.concatenate(seen, axis=0) >= 0, p, 0.0)
            ds = (p * (dp - delta)).astype(bf16)
            dv[at, :] += dot(p.astype(bf16), do, NN)
            dk[at, :] += dot(ds, q, NN)
            part = dot(kt[:, at], ds, NN)
            total = part if total is None else total + part
        dq[...] += total

    def group(g, carry):
        dq[...] = jnp.zeros_like(dq)
        whole = below[g] // WIDE
        pairs = whole // UNROLL

        def step(i, carry):
            unit(g, i * UNROLL, UNROLL, WIDE, False)
            return carry

        def single(i, carry):
            unit(g, i, 1, WIDE, False)
            return carry

        lax.fori_loop(0, pairs, step, 0)
        lax.fori_loop(pairs * UNROLL, whole, single, 0)

        rest = below[g] + own[g] - whole * WIDE

        @pl.when((rest > 0) & (rest <= WIDE // 2))
        def _():
            unit(g, whole, 1, WIDE // 2, True)

        @pl.when(rest > WIDE // 2)
        def _():
            unit(g, whole, 1, WIDE, True)

        @pl.when(g < half)
        def _():
            for j in range(0, rows, width):
                near_ref[g, j : j + width, :] = dq[:, j : j + width].T

        @pl.when(g >= half)
        def _():
            for j in range(0, rows, width):
                far_ref[g - half, j : j + width, :] = dq[:, j : j + width].T.astype(far_ref.dtype)

        return carry

    half = groups // 2
    lax.fori_loop(0, groups, group, 0)
    for r in range(blocks):
        at = pl.ds(r * span, span)
        dkv_ref[order[r]] = jnp.concatenate([dk[at, :], dv[at, :]], axis=1).astype(dkv_ref.dtype)


def attend(tables, kv, payloads, dq_type, dkv_type):
    counts = tuple(p.shape[0] for p in payloads)
    groups = sum(counts)
    rows = (payloads[0].shape[1] - STAT_ROWS) // 2
    blocks, span, width = kv.shape
    width = width // 2
    vmem = pl.BlockSpec(memory_space=pltpu.VMEM)
    smem = pl.BlockSpec(memory_space=pltpu.SMEM)
    scale = 1.0 / math.sqrt(width)
    pairs = groups * rows * blocks * span // 2
    return pl.pallas_call(
        functools.partial(kernel, counts, scale),
        out_shape=(
            jax.ShapeDtypeStruct((groups // 2, rows, width), f32),
            jax.ShapeDtypeStruct((groups // 2, rows, width), dq_type),
            jax.ShapeDtypeStruct(kv.shape, dkv_type),
        ),
        in_specs=[smem] * len(tables) + [vmem] + [pl.BlockSpec(memory_space=pltpu.MemorySpace.HBM)] * len(payloads),
        out_specs=(vmem, vmem, vmem),
        scratch_shapes=[
            pltpu.VMEM((groups, *payloads[0].shape[1:]), bf16),
            pltpu.VMEM((groups, 2, rows), f32),
            pltpu.VMEM((blocks * span, width), bf16),
            pltpu.VMEM((blocks * span, width), bf16),
            pltpu.VMEM((width, blocks * span), bf16),
            pltpu.VMEM((blocks * span, width), f32),
            pltpu.VMEM((blocks * span, width), f32),
            pltpu.VMEM((width, rows), f32),
            pltpu.SemaphoreType.DMA((len(payloads),)),
        ],
        cost_estimate=pl.CostEstimate(
            flops=pairs * width * 20, transcendentals=pairs, bytes_accessed=8 << 20
        ),
        compiler_params=pltpu.CompilerParams(vmem_limit_bytes=40 << 20),
        name="attend",
    )(*tables, kv, *payloads)


def prepare_kernel(q_ref, do_ref, o_ref, log_ref, k_ref, v_ref, mine_ref, kv_ref):
    heads, tokens, width = q_ref.shape
    span = tokens // 2
    rows = heads * span
    for j in range(kv_ref.shape[0]):
        kv_ref[j, :, :width] = k_ref[...]
        kv_ref[j, :, width:] = v_ref[...]
    ones = jnp.ones((8, width), bf16)
    log_norm = log_ref[...] * LOG2E
    turned = pltpu.roll(log_norm, span, 1)
    lower = lax.broadcasted_iota(jnp.int32, (1, tokens), 1) < span

    def terms(x):
        high = x.astype(bf16)
        rest = x - high.astype(f32)
        middle = rest.astype(bf16)
        low = (rest - middle.astype(f32)).astype(bf16)
        return [high.astype(f32), middle.astype(f32), low.astype(f32)]

    for s in range(2):
        at = slice(s * span, (s + 1) * span)
        mine_ref[s, :rows, :] = q_ref[:, at, :].reshape(rows, width)
        do = do_ref[:, at, :].reshape(rows, width)
        mine_ref[s, rows : 2 * rows, :] = do
        both = do.astype(f32) * o_ref[:, at, :].reshape(rows, width).astype(f32)
        high = both.astype(bf16)
        low = (both - high.astype(f32)).astype(bf16)
        delta = dot(ones, high, NT) + dot(ones, low, NT)
        delta = jnp.concatenate(
            [delta[0:1, j : j + width] for j in range(0, rows, width)], axis=0
        )
        first, second = (log_norm, turned) if s == 0 else (turned, log_norm)
        norms = jnp.concatenate(
            [
                jnp.where(lower, first[j : j + 1], second[j + 1 : j + 2])
                for j in range(0, heads, 2)
            ],
            axis=0,
        )
        pieces = terms(norms) + terms(delta)
        filled = sum(p.shape[0] for p in pieces)
        pieces.append(jnp.zeros((STAT_ROWS - filled, width), f32))
        mine_ref[s, 2 * rows :, :] = jnp.concatenate(pieces, axis=0).astype(bf16)


def prepare(q, do, o, log_sums, k, v, copies):
    heads, tokens, width = q.shape
    vmem = pl.BlockSpec(memory_space=pltpu.VMEM)
    return pl.pallas_call(
        prepare_kernel,
        out_shape=(
            jax.ShapeDtypeStruct((2, heads * tokens + STAT_ROWS, width), bf16),
            jax.ShapeDtypeStruct((copies, tokens, 2 * width), bf16),
        ),
        in_specs=[vmem] * 6,
        out_specs=(vmem, vmem),
        name="prepare",
    )(q, do, o, log_sums, k, v)


def lookup(table, ids):
    hits = ids[:, None] == jnp.arange(table.shape[0], dtype=jnp.int32)[None, :]
    return jnp.sum(jnp.where(hits, table[None, :], 0), axis=1)


def rank(zh, zl, xl, c, yh, yl, xh):
    out = 0
    for bit in (zh, zl, xl, c, yh, yl, xh):
        out = out * 2 + bit
    return out


def x_shift(a, by):
    at = lambda x: (x % 2) * 2 + x // 2
    return lax.ppermute(a, ("xl", "xh"), [(at(x), at((x + by) % 4)) for x in range(4)])


def swap(a):
    return lax.ppermute(a, "c", [(0, 1), (1, 0)])


def body(q, k, v, o, do, log_sums, span_order):
    heads, tokens, width = q.shape
    span = tokens // 2
    rows = heads * span
    scale = 1.0 / math.sqrt(width)
    zh, zl, xl, c, yh, yl, xh = [lax.axis_index(a) for a in AXES]
    x = xh * 2 + xl

    mine, kv = prepare(q, do, o, log_sums, k, v, 16)
    right = x_shift(mine, 1)
    left = x_shift(mine, -1)
    across = x_shift(mine, 2)
    kv = lax.all_to_all(kv, KV_AXES, 0, 0, tiled=True).reshape(32, span, 2 * width)
    near = (mine, right, left, across)
    far = tuple(swap(a) for a in near)

    i16 = jnp.arange(16, dtype=jnp.int32)
    kv_ids = rank(i16 // 8, i16 // 2 % 2, xl, c, i16 % 2, i16 // 4 % 2, xh)
    q_ids = []
    for cc in (c, 1 - c):
        for shift in (0, 3, 1, 2):
            xx = (x + shift) & 3
            q_ids.append(rank(zh, zl, xx & 1, cc, yh, yl, xx >> 1))
    ids = jnp.concatenate([kv_ids, jnp.stack(q_ids)])
    ids = (ids[:, None] * 2 + jnp.arange(2, dtype=jnp.int32)[None, :]).reshape(48)
    pos = lookup(span_order, ids)
    kv_pos, q_pos = pos[:32], pos[32:]
    place = jnp.sum((kv_pos[None, :] < kv_pos[:, None]).astype(jnp.int32), axis=1)
    hit = place[:, None] == jnp.arange(32, dtype=jnp.int32)[None, :]
    order = jnp.sum(jnp.where(hit, jnp.arange(32, dtype=jnp.int32)[:, None], 0), axis=0)
    sorted_pos = jnp.sum(jnp.where(hit, kv_pos[:, None], 0), axis=0)
    below = jnp.sum((kv_pos[None, :] < q_pos[:, None]).astype(jnp.int32), axis=1)
    own = jnp.sum((kv_pos[None, :] == q_pos[:, None]).astype(jnp.int32), axis=1)

    tables = (order, sorted_pos, q_pos, below, own)
    dq, dq_far, dkv = attend(tables, kv, near + far, bf16, bf16)

    dkv = lax.all_to_all(dkv.reshape(16, tokens, 2 * width), KV_AXES, 0, 0, tiled=True)
    dkv = jnp.sum(dkv.astype(f32), axis=0)
    dk = (dkv[:, :width] * scale).astype(bf16)
    dv = dkv[:, width:].astype(bf16)

    dq = dq + swap(dq_far).astype(f32)
    out = dq.astype(bf16)
    parts = [x_shift(out[2:4], -1), x_shift(out[4:6], 1), x_shift(out[6:8], 2)]
    dq = (dq[:2] + sum(p.astype(f32) for p in parts)) * scale
    dq = dq.reshape(2, heads, span, width).transpose(1, 0, 2, 3).reshape(heads, tokens, width)
    return dq.astype(bf16), dk, dv


def solution(mesh):
    fine = Mesh(mesh.devices.reshape((2,) * 7), AXES)
    return jax.shard_map(
        body,
        mesh=fine,
        in_specs=(
            P(None, AXES, None),
            P(AXES, None),
            P(AXES, None),
            P(None, AXES, None),
            P(None, AXES, None),
            P(None, AXES),
            P(),
        ),
        out_specs=(P(None, AXES, None), P(AXES, None), P(AXES, None)),
        check_vma=False,
    )
```

```python
import functools
import math

import jax
import jax.numpy as jnp
from jax import lax
from jax.experimental import pallas as pl
from jax.experimental.pallas import tpu as pltpu
from jax.sharding import Mesh
from jax.sharding import PartitionSpec as P


f32 = jnp.float32
bf16 = jnp.bfloat16
NT = (((1,), (1,)), ((), ()))
NN = (((1,), (0,)), ((), ()))
LOG2E = 1.0 / math.log(2.0)
AXES = ("zh", "zl", "xl", "c", "yh", "yl", "xh")
KV_AXES = ("zl", "yl", "zh", "yh")
WIDE = 4
UNROLL = 2
LIMIT = 24
STAT_ROWS = 32


def dot(a, b, dims):
    return lax.dot_general(a, b, dims, preferred_element_type=f32)


def kernel(first, last, counts, near, scale, order, sorted_pos, query_block, below, own, *rest):
    if first:
        kv_ref, rest = rest[0], rest[1:]
    else:
        (ks, vs, kt, dk_ref, dv_ref), rest = rest[:5], rest[5:]
    payloads, rest = rest[: len(counts)], rest[len(counts) :]
    near_ref = far_ref = None
    if near:
        near_ref, rest = rest[0], rest[1:]
    if near < sum(counts):
        far_ref, rest = rest[0], rest[1:]
    if first:
        (ks, vs, kt), rest = rest[:3], rest[3:]
    if last:
        dkv_ref, rest = rest[0], rest[1:]
    dk, dv, qd, st, dq = rest
    groups, _, width = qd.shape
    rows = st.shape[2]
    blocks = order.shape[0]
    span = ks.shape[0] // blocks
    chunk = WIDE * span
    if first:
        for r in range(blocks):
            block = kv_ref[order[r]]
            ks[r * span : (r + 1) * span, :] = block[:, :width]
            vs[r * span : (r + 1) * span, :] = block[:, width:]
        for r in range(0, blocks * span, chunk):
            kt[:, r : r + chunk] = ks[r : r + chunk, :].T
        dk[...] = jnp.zeros_like(dk)
        dv[...] = jnp.zeros_like(dv)
    else:
        dk[...] = dk_ref[...]
        dv[...] = dv_ref[...]
    lines = rows // width
    g = 0
    for ref, count in zip(payloads, counts):
        for i in range(count):
            qd[g] = ref[i, : 2 * rows, :]
            terms = ref[i, 2 * rows :, :].astype(f32)
            for kind in range(2):
                t = terms[kind * 3 * lines :]
                t = t[:lines] + t[lines : 2 * lines] + t[2 * lines : 3 * lines]
                st[g, kind : kind + 1, :] = jnp.concatenate(
                    [t[j : j + 1] for j in range(lines)], axis=1
                )
            g += 1

    def unit(g, first, count, size, masked):
        q, do = qd[g, :rows, :], qd[g, rows : 2 * rows, :]
        log_norm, delta = st[g, 0:1, :], st[g, 1:2, :]
        total = None
        for n in range(count):
            at = pl.ds(pl.multiple_of((first + n) * chunk, chunk), size * span)
            k, v = ks[at, :], vs[at, :]
            s = dot(k, q, NT)
            dp = dot(v, do, NT)
            p = jnp.exp2(s * (scale * LOG2E) - log_norm)
            if masked:
                lead = lax.rem(lax.broadcasted_iota(jnp.int32, (span, rows), 1), span)
                lead = lead - lax.broadcasted_iota(jnp.int32, (span, rows), 0)
                seen = [
                    lead + (query_block[g] - sorted_pos[(first + n) * WIDE + j]) * span
                    for j in range(size)
                ]
                p = jnp.where(jnp.concatenate(seen, axis=0) >= 0, p, 0.0)
            ds = (p * (dp - delta)).astype(bf16)
            dv[at, :] += dot(p.astype(bf16), do, NN)
            dk[at, :] += dot(ds, q, NN)
            part = dot(kt[:, at], ds, NN)
            total = part if total is None else total + part
        dq[...] += total

    def group(g, carry):
        dq[...] = jnp.zeros_like(dq)
        whole = below[g] // WIDE
        pairs = whole // UNROLL

        def step(i, carry):
            unit(g, i * UNROLL, UNROLL, WIDE, False)
            return carry

        def single(i, carry):
            unit(g, i, 1, WIDE, False)
            return carry

        lax.fori_loop(0, pairs, step, 0)
        lax.fori_loop(pairs * UNROLL, whole, single, 0)

        rest = below[g] + own[g] - whole * WIDE

        @pl.when((rest > 0) & (rest <= WIDE // 2))
        def _():
            unit(g, whole, 1, WIDE // 2, True)

        @pl.when(rest > WIDE // 2)
        def _():
            unit(g, whole, 1, WIDE, True)

        def store_near():
            for j in range(0, rows, width):
                near_ref[g, j : j + width, :] = dq[:, j : j + width].T

        def store_far():
            for j in range(0, rows, width):
                far_ref[g - near, j : j + width, :] = dq[:, j : j + width].T.astype(bf16)

        if far_ref is None:
            store_near()
        elif near_ref is None:
            store_far()
        else:
            pl.when(g < near)(store_near)
            pl.when(g >= near)(store_far)
        return carry

    lax.fori_loop(0, groups, group, 0)
    if last:
        for r in range(blocks):
            at = pl.ds(r * span, span)
            dkv_ref[order[r]] = jnp.concatenate([dk[at, :], dv[at, :]], axis=1).astype(
                dkv_ref.dtype
            )


def attend(tables, state, payloads, near, first, last):
    counts = tuple(p.shape[0] for p in payloads)
    groups = sum(counts)
    width = payloads[0].shape[2]
    rows = (payloads[0].shape[1] - STAT_ROWS) // 2
    blocks = tables[0].shape[0]
    if first:
        (kv,) = state
        keys = blocks * kv.shape[1]
    else:
        keys = state[0].shape[0]
    span = keys // blocks
    vmem = pl.BlockSpec(memory_space=pltpu.VMEM)
    smem = pl.BlockSpec(memory_space=pltpu.SMEM)
    scale = 1.0 / math.sqrt(width)
    pairs = groups * rows * keys // 2
    totals = [jax.ShapeDtypeStruct((keys, width), f32)] * 2
    out_shape = []
    if near:
        out_shape.append(jax.ShapeDtypeStruct((near, rows, width), f32))
    if near < groups:
        out_shape.append(jax.ShapeDtypeStruct((groups - near, rows, width), bf16))
    scratch = [
        pltpu.VMEM((groups, 2 * rows, width), bf16),
        pltpu.VMEM((groups, 2, rows), f32),
        pltpu.VMEM((width, rows), f32),
    ]
    if first:
        out_shape += [
            jax.ShapeDtypeStruct((keys, width), bf16),
            jax.ShapeDtypeStruct((keys, width), bf16),
            jax.ShapeDtypeStruct((width, keys), bf16),
        ]
    if last:
        out_shape.append(jax.ShapeDtypeStruct((blocks, span, 2 * width), bf16))
        scratch = [pltpu.VMEM((keys, width), f32)] * 2 + scratch
    else:
        out_shape += totals
    out_specs = [vmem] * len(out_shape)
    return pl.pallas_call(
        functools.partial(kernel, first, last, counts, near, scale),
        out_shape=tuple(out_shape),
        in_specs=[smem] * len(tables) + [vmem] * (len(state) + len(payloads)),
        out_specs=tuple(out_specs),
        scratch_shapes=scratch,
        cost_estimate=pl.CostEstimate(
            flops=pairs * width * 20, transcendentals=pairs, bytes_accessed=8 << 20
        ),
        compiler_params=pltpu.CompilerParams(vmem_limit_bytes=LIMIT << 20),
    )(*tables, *state, *payloads)


def copies_kernel(k_ref, v_ref, kv_ref, tile, sems):
    width = k_ref.shape[1]
    count = kv_ref.shape[0]
    reads = [
        pltpu.make_async_copy(ref, tile.at[:, pl.ds(n * width, width)], sems.at[count + n])
        for n, ref in enumerate((k_ref, v_ref))
    ]
    for copy in reads:
        copy.start()
    for copy in reads:
        copy.wait()
    writes = [pltpu.make_async_copy(tile, kv_ref.at[j], sems.at[j]) for j in range(count)]
    for copy in writes:
        copy.start()
    for copy in writes:
        copy.wait()


def copy_out(k, v, count):
    tokens, width = k.shape
    hbm = pltpu.MemorySpace.HBM
    spec = pl.BlockSpec(memory_space=hbm)
    return pl.pallas_call(
        copies_kernel,
        out_shape=jax.ShapeDtypeStruct((count, tokens, 2 * width), k.dtype),
        in_specs=[spec, spec],
        out_specs=spec,
        scratch_shapes=[
            pltpu.VMEM((tokens, 2 * width), k.dtype),
            pltpu.SemaphoreType.DMA((count + 2,)),
        ],
        compiler_params=pltpu.CompilerParams(vmem_limit_bytes=8 << 20),
        name="copies",
    )(*(pltpu.with_memory_space_constraint(a, hbm) for a in (k, v)))


def prepare_kernel(q_ref, do_ref, o_ref, log_ref, mine_ref):
    heads, tokens, width = q_ref.shape
    span = tokens // 2
    rows = heads * span
    ones = jnp.ones((8, width), bf16)
    log_norm = log_ref[...] * LOG2E
    turned = pltpu.roll(log_norm, span, 1)
    lower = lax.broadcasted_iota(jnp.int32, (1, tokens), 1) < span

    def terms(x):
        high = x.astype(bf16)
        rest = x - high.astype(f32)
        middle = rest.astype(bf16)
        low = (rest - middle.astype(f32)).astype(bf16)
        return [high.astype(f32), middle.astype(f32), low.astype(f32)]

    for s in range(2):
        at = slice(s * span, (s + 1) * span)
        mine_ref[s, :rows, :] = q_ref[:, at, :].reshape(rows, width)
        do = do_ref[:, at, :].reshape(rows, width)
        mine_ref[s, rows : 2 * rows, :] = do
        both = do.astype(f32) * o_ref[:, at, :].reshape(rows, width).astype(f32)
        high = both.astype(bf16)
        low = (both - high.astype(f32)).astype(bf16)
        delta = dot(ones, high, NT) + dot(ones, low, NT)
        delta = jnp.concatenate(
            [delta[0:1, j : j + width] for j in range(0, rows, width)], axis=0
        )
        first, second = (log_norm, turned) if s == 0 else (turned, log_norm)
        norms = jnp.concatenate(
            [
                jnp.where(lower, first[j : j + 1], second[j + 1 : j + 2])
                for j in range(0, heads, 2)
            ],
            axis=0,
        )
        pieces = terms(norms) + terms(delta)
        filled = sum(p.shape[0] for p in pieces)
        pieces.append(jnp.zeros((STAT_ROWS - filled, width), f32))
        mine_ref[s, 2 * rows :, :] = jnp.concatenate(pieces, axis=0).astype(bf16)


def local_call(function, out_shape, *args):
    vmem = pl.BlockSpec(memory_space=pltpu.VMEM)
    many = isinstance(out_shape, tuple)
    return pl.pallas_call(
        function,
        out_shape=out_shape,
        in_specs=[vmem] * len(args),
        out_specs=(vmem,) * len(out_shape) if many else vmem,
        compiler_params=pltpu.CompilerParams(vmem_limit_bytes=8 << 20),
    )(*args)


def finish_kernel(scale, parts_ref, dk_ref, dv_ref):
    width = dk_ref.shape[1]
    total = parts_ref[0].astype(f32)
    for j in range(1, parts_ref.shape[0]):
        total = total + parts_ref[j].astype(f32)
    dk_ref[...] = (total[:, :width] * scale).astype(bf16)
    dv_ref[...] = total[:, width:].astype(bf16)


def finish_dq_kernel(scale, own_ref, *rest):
    parts, dq_ref = rest[:-1], rest[-1]
    heads, tokens, width = dq_ref.shape
    span = tokens // 2
    for s in range(2):
        total = own_ref[s]
        for ref in parts:
            total = total + ref[s].astype(f32)
        total = (total * scale).astype(bf16)
        dq_ref[:, s * span : (s + 1) * span, :] = total.reshape(heads, span, width)


def lookup(table, ids):
    hits = ids[:, None] == jnp.arange(table.shape[0], dtype=jnp.int32)[None, :]
    return jnp.sum(jnp.where(hits, table[None, :], 0), axis=1)


def rank(zh, zl, xl, c, yh, yl, xh):
    out = 0
    for bit in (zh, zl, xl, c, yh, yl, xh):
        out = out * 2 + bit
    return out


def x_shift(a, by):
    at = lambda x: (x % 2) * 2 + x // 2
    return lax.ppermute(a, ("xl", "xh"), [(at(x), at((x + by) % 4)) for x in range(4)])


def swap(a):
    return lax.ppermute(a, "c", [(0, 1), (1, 0)])


def spread(a):
    return lax.all_to_all(a, KV_AXES, 0, 0, tiled=True)


def body(q, k, v, o, do, log_sums, span_order):
    heads, tokens, width = q.shape
    span = tokens // 2
    scale = 1.0 / math.sqrt(width)
    zh, zl, xl, c, yh, yl, xh = [lax.axis_index(a) for a in AXES]
    x = xh * 2 + xl

    kv = copy_out(k, v, 16)
    payload = jax.ShapeDtypeStruct((2, heads * tokens + STAT_ROWS, width), bf16)
    mine = local_call(prepare_kernel, payload, q, do, o, log_sums)
    kv = spread(kv).reshape(32, span, 2 * width)
    right = x_shift(mine, 1)
    left = x_shift(mine, -1)
    across = x_shift(mine, 2)

    i16 = jnp.arange(16, dtype=jnp.int32)
    bits = {axis: (i16 >> (3 - n)) & 1 for n, axis in enumerate(KV_AXES)}
    kv_ids = rank(bits["zh"], bits["zl"], xl, c, bits["yh"], bits["yl"], xh)
    q_ids = []
    for near_shifts, far_shifts in (((0,), (0,)), ((3, 1, 2), ()), ((), (3, 1, 2))):
        chosen = [(c, shift) for shift in near_shifts] + [(1 - c, shift) for shift in far_shifts]
        for cc, shift in chosen:
            xx = (x + shift) & 3
            q_ids.append(rank(zh, zl, xx & 1, cc, yh, yl, xx >> 1))
    ids = jnp.concatenate([kv_ids, jnp.stack(q_ids)])
    ids = (ids[:, None] * 2 + jnp.arange(2, dtype=jnp.int32)[None, :]).reshape(48)
    pos = lookup(span_order, ids)
    kv_pos, q_pos = pos[:32], pos[32:]
    place = jnp.sum((kv_pos[None, :] < kv_pos[:, None]).astype(jnp.int32), axis=1)
    hit = place[:, None] == jnp.arange(32, dtype=jnp.int32)[None, :]
    order = jnp.sum(jnp.where(hit, jnp.arange(32, dtype=jnp.int32)[:, None], 0), axis=0)
    sorted_pos = jnp.sum(jnp.where(hit, kv_pos[:, None], 0), axis=0)
    below = jnp.sum((kv_pos[None, :] < q_pos[:, None]).astype(jnp.int32), axis=1)
    own = jnp.sum((kv_pos[None, :] == q_pos[:, None]).astype(jnp.int32), axis=1)

    def tables(start, count):
        at = slice(start, start + count)
        return (order, sorted_pos, q_pos[at], below[at], own[at])

    first = (mine, swap(mine))
    dq, dq_far, *state = attend(tables(0, 4), (kv,), first, 2, True, False)
    near = (right, left, across)
    far = (swap(right), swap(left), swap(across))
    dq_near, dk, dv = attend(tables(4, 6), state, near, 6, False, False)
    state = (*state[:3], dk, dv)
    dq_back, dkv = attend(tables(10, 6), state, far, 0, False, True)
    dq_own = swap(dq_far)
    out = (dq_near + swap(dq_back).astype(f32)).astype(bf16)

    dkv = spread(dkv.reshape(16, tokens, 2 * width))
    shape = jax.ShapeDtypeStruct((tokens, width), bf16)
    dk, dv = local_call(functools.partial(finish_kernel, scale), (shape, shape), dkv)
    parts = [x_shift(out[:2], -1), x_shift(out[2:4], 1), x_shift(out[4:], 2)]
    shape = jax.ShapeDtypeStruct((heads, tokens, width), bf16)
    finish_dq = functools.partial(finish_dq_kernel, scale)
    return local_call(finish_dq, shape, dq, dq_own, *parts), dk, dv


def solution(mesh):
    fine = Mesh(mesh.devices.reshape((2,) * 7), AXES)
    return jax.shard_map(
        body,
        mesh=fine,
        in_specs=(
            P(None, AXES, None),
            P(AXES, None),
            P(AXES, None),
            P(None, AXES, None),
            P(None, AXES, None),
            P(None, AXES),
            P(),
        ),
        out_specs=(P(None, AXES, None), P(AXES, None), P(AXES, None)),
        check_vma=False,
    )
```

```python
import functools
import math

import jax
import jax.numpy as jnp
from jax import lax
from jax.experimental import pallas as pl
from jax.experimental.pallas import tpu as pltpu
from jax.sharding import Mesh
from jax.sharding import PartitionSpec as P


f32 = jnp.float32
bf16 = jnp.bfloat16
NT = (((1,), (1,)), ((), ()))
NN = (((1,), (0,)), ((), ()))
LOG2E = 1.0 / math.log(2.0)
AXES = ("zh", "zl", "xl", "c", "yh", "yl", "xh")
KV_AXES = ("zl", "yl", "zh", "yh")
WIDE = 4
UNROLL = 2
LIMIT = 24
STAT_ROWS = 32


def dot(a, b, dims):
    return lax.dot_general(a, b, dims, preferred_element_type=f32)


def kernel(first, last, counts, near, scale, order, sorted_pos, query_block, below, own, *rest):
    if first:
        kv_ref, rest = rest[0], rest[1:]
    else:
        (ks, vs, kt, dk_ref, dv_ref), rest = rest[:5], rest[5:]
    payloads, rest = rest[: len(counts)], rest[len(counts) :]
    near_ref = far_ref = None
    if near:
        near_ref, rest = rest[0], rest[1:]
    if near < sum(counts):
        far_ref, rest = rest[0], rest[1:]
    if first:
        (ks, vs, kt), rest = rest[:3], rest[3:]
    if last:
        dkv_ref, rest = rest[0], rest[1:]
    dk, dv, qd, st, dq = rest
    groups, _, width = qd.shape
    rows = st.shape[2]
    blocks = order.shape[0]
    span = ks.shape[0] // blocks
    chunk = WIDE * span
    if first:
        for r in range(blocks):
            block = kv_ref[order[r]]
            ks[r * span : (r + 1) * span, :] = block[:, :width]
            vs[r * span : (r + 1) * span, :] = block[:, width:]
        for r in range(0, blocks * span, chunk):
            kt[:, r : r + chunk] = ks[r : r + chunk, :].T
        dk[...] = jnp.zeros_like(dk)
        dv[...] = jnp.zeros_like(dv)
    else:
        dk[...] = dk_ref[...]
        dv[...] = dv_ref[...]
    lines = rows // width
    g = 0
    for ref, count in zip(payloads, counts):
        for i in range(count):
            qd[g] = ref[i, : 2 * rows, :]
            terms = ref[i, 2 * rows :, :].astype(f32)
            for kind in range(2):
                t = terms[kind * 3 * lines :]
                t = t[:lines] + t[lines : 2 * lines] + t[2 * lines : 3 * lines]
                st[g, kind : kind + 1, :] = jnp.concatenate(
                    [t[j : j + 1] for j in range(lines)], axis=1
                )
            g += 1

    def unit(g, first, count, size, masked):
        q, do = qd[g, :rows, :], qd[g, rows : 2 * rows, :]
        log_norm, delta = st[g, 0:1, :], st[g, 1:2, :]
        total = None
        for n in range(count):
            at = pl.ds(pl.multiple_of((first + n) * chunk, chunk), size * span)
            k, v = ks[at, :], vs[at, :]
            s = dot(k, q, NT)
            dp = dot(v, do, NT)
            p = jnp.exp2(s * (scale * LOG2E) - log_norm)
            if masked:
                lead = lax.rem(lax.broadcasted_iota(jnp.int32, (span, rows), 1), span)
                lead = lead - lax.broadcasted_iota(jnp.int32, (span, rows), 0)
                seen = [
                    lead + (query_block[g] - sorted_pos[(first + n) * WIDE + j]) * span
                    for j in range(size)
                ]
                p = jnp.where(jnp.concatenate(seen, axis=0) >= 0, p, 0.0)
            ds = (p * (dp - delta)).astype(bf16)
            dv[at, :] += dot(p.astype(bf16), do, NN)
            dk[at, :] += dot(ds, q, NN)
            part = dot(kt[:, at], ds, NN)
            total = part if total is None else total + part
        dq[...] += total

    def group(g, carry):
        dq[...] = jnp.zeros_like(dq)
        whole = below[g] // WIDE
        pairs = whole // UNROLL

        def step(i, carry):
            unit(g, i * UNROLL, UNROLL, WIDE, False)
            return carry

        def single(i, carry):
            unit(g, i, 1, WIDE, False)
            return carry

        lax.fori_loop(0, pairs, step, 0)
        lax.fori_loop(pairs * UNROLL, whole, single, 0)

        rest = below[g] + own[g] - whole * WIDE

        @pl.when((rest > 0) & (rest <= WIDE // 2))
        def _():
            unit(g, whole, 1, WIDE // 2, True)

        @pl.when(rest > WIDE // 2)
        def _():
            unit(g, whole, 1, WIDE, True)

        def store_near():
            for j in range(0, rows, width):
                near_ref[g, j : j + width, :] = dq[:, j : j + width].T

        def store_far():
            for j in range(0, rows, width):
                far_ref[g - near, j : j + width, :] = dq[:, j : j + width].T.astype(bf16)

        if far_ref is None:
            store_near()
        elif near_ref is None:
            store_far()
        else:
            pl.when(g < near)(store_near)
            pl.when(g >= near)(store_far)
        return carry

    lax.fori_loop(0, groups, group, 0)
    if last:
        for r in range(blocks):
            at = pl.ds(r * span, span)
            dkv_ref[order[r]] = jnp.concatenate([dk[at, :], dv[at, :]], axis=1).astype(
                dkv_ref.dtype
            )


def attend(tables, state, payloads, near, first, last):
    counts = tuple(p.shape[0] for p in payloads)
    groups = sum(counts)
    width = payloads[0].shape[2]
    rows = (payloads[0].shape[1] - STAT_ROWS) // 2
    blocks = tables[0].shape[0]
    if first:
        (kv,) = state
        keys = blocks * kv.shape[1]
    else:
        keys = state[0].shape[0]
    span = keys // blocks
    vmem = pl.BlockSpec(memory_space=pltpu.VMEM)
    smem = pl.BlockSpec(memory_space=pltpu.SMEM)
    scale = 1.0 / math.sqrt(width)
    pairs = groups * rows * keys // 2
    totals = [jax.ShapeDtypeStruct((keys, width), f32)] * 2
    out_shape = []
    if near:
        out_shape.append(jax.ShapeDtypeStruct((near, rows, width), f32))
    if near < groups:
        out_shape.append(jax.ShapeDtypeStruct((groups - near, rows, width), bf16))
    scratch = [
        pltpu.VMEM((groups, 2 * rows, width), bf16),
        pltpu.VMEM((groups, 2, rows), f32),
        pltpu.VMEM((width, rows), f32),
    ]
    if first:
        out_shape += [
            jax.ShapeDtypeStruct((keys, width), bf16),
            jax.ShapeDtypeStruct((keys, width), bf16),
            jax.ShapeDtypeStruct((width, keys), bf16),
        ]
    if last:
        out_shape.append(jax.ShapeDtypeStruct((blocks, span, 2 * width), bf16))
        scratch = [pltpu.VMEM((keys, width), f32)] * 2 + scratch
    else:
        out_shape += totals
    out_specs = [vmem] * len(out_shape)
    return pl.pallas_call(
        functools.partial(kernel, first, last, counts, near, scale),
        out_shape=tuple(out_shape),
        in_specs=[smem] * len(tables) + [vmem] * (len(state) + len(payloads)),
        out_specs=tuple(out_specs),
        scratch_shapes=scratch,
        cost_estimate=pl.CostEstimate(
            flops=pairs * width * 20, transcendentals=pairs, bytes_accessed=8 << 20
        ),
        compiler_params=pltpu.CompilerParams(vmem_limit_bytes=LIMIT << 20),
    )(*tables, *state, *payloads)


def prepare_kernel(q_ref, do_ref, o_ref, log_ref, k_ref, v_ref, mine_ref, kv_ref):
    heads, tokens, width = q_ref.shape
    span = tokens // 2
    rows = heads * span
    for j in range(kv_ref.shape[0]):
        kv_ref[j, :, :width] = k_ref[...]
        kv_ref[j, :, width:] = v_ref[...]
    ones = jnp.ones((8, width), bf16)
    log_norm = log_ref[...] * LOG2E
    turned = pltpu.roll(log_norm, span, 1)
    lower = lax.broadcasted_iota(jnp.int32, (1, tokens), 1) < span

    def terms(x):
        high = x.astype(bf16)
        rest = x - high.astype(f32)
        middle = rest.astype(bf16)
        low = (rest - middle.astype(f32)).astype(bf16)
        return [high.astype(f32), middle.astype(f32), low.astype(f32)]

    for s in range(2):
        at = slice(s * span, (s + 1) * span)
        mine_ref[s, :rows, :] = q_ref[:, at, :].reshape(rows, width)
        do = do_ref[:, at, :].reshape(rows, width)
        mine_ref[s, rows : 2 * rows, :] = do
        both = do.astype(f32) * o_ref[:, at, :].reshape(rows, width).astype(f32)
        high = both.astype(bf16)
        low = (both - high.astype(f32)).astype(bf16)
        delta = dot(ones, high, NT) + dot(ones, low, NT)
        delta = jnp.concatenate(
            [delta[0:1, j : j + width] for j in range(0, rows, width)], axis=0
        )
        first, second = (log_norm, turned) if s == 0 else (turned, log_norm)
        norms = jnp.concatenate(
            [
                jnp.where(lower, first[j : j + 1], second[j + 1 : j + 2])
                for j in range(0, heads, 2)
            ],
            axis=0,
        )
        pieces = terms(norms) + terms(delta)
        filled = sum(p.shape[0] for p in pieces)
        pieces.append(jnp.zeros((STAT_ROWS - filled, width), f32))
        mine_ref[s, 2 * rows :, :] = jnp.concatenate(pieces, axis=0).astype(bf16)


def local_call(function, out_shape, *args, limit=8):
    vmem = pl.BlockSpec(memory_space=pltpu.VMEM)
    many = isinstance(out_shape, tuple)
    return pl.pallas_call(
        function,
        out_shape=out_shape,
        in_specs=[vmem] * len(args),
        out_specs=(vmem,) * len(out_shape) if many else vmem,
        compiler_params=pltpu.CompilerParams(vmem_limit_bytes=limit << 20),
    )(*args)


def finish_kernel(scale, parts_ref, dk_ref, dv_ref):
    width = dk_ref.shape[1]
    total = parts_ref[0].astype(f32)
    for j in range(1, parts_ref.shape[0]):
        total = total + parts_ref[j].astype(f32)
    dk_ref[...] = (total[:, :width] * scale).astype(bf16)
    dv_ref[...] = total[:, width:].astype(bf16)


def finish_dq_kernel(scale, own_ref, *rest):
    parts, dq_ref = rest[:-1], rest[-1]
    heads, tokens, width = dq_ref.shape
    span = tokens // 2
    for s in range(2):
        total = own_ref[s]
        for ref in parts:
            total = total + ref[s].astype(f32)
        total = (total * scale).astype(bf16)
        dq_ref[:, s * span : (s + 1) * span, :] = total.reshape(heads, span, width)


def lookup(table, ids):
    hits = ids[:, None] == jnp.arange(table.shape[0], dtype=jnp.int32)[None, :]
    return jnp.sum(jnp.where(hits, table[None, :], 0), axis=1)


def rank(zh, zl, xl, c, yh, yl, xh):
    out = 0
    for bit in (zh, zl, xl, c, yh, yl, xh):
        out = out * 2 + bit
    return out


def x_shift(a, by):
    at = lambda x: (x % 2) * 2 + x // 2
    return lax.ppermute(a, ("xl", "xh"), [(at(x), at((x + by) % 4)) for x in range(4)])


def swap(a):
    return lax.ppermute(a, "c", [(0, 1), (1, 0)])


def spread(a):
    return lax.all_to_all(a, KV_AXES, 0, 0, tiled=True)


def body(q, k, v, o, do, log_sums, span_order):
    heads, tokens, width = q.shape
    span = tokens // 2
    scale = 1.0 / math.sqrt(width)
    zh, zl, xl, c, yh, yl, xh = [lax.axis_index(a) for a in AXES]
    x = xh * 2 + xl

    payload = jax.ShapeDtypeStruct((2, heads * tokens + STAT_ROWS, width), bf16)
    copies = jax.ShapeDtypeStruct((16, tokens, 2 * width), bf16)
    mine, kv = local_call(
        prepare_kernel, (payload, copies), q, do, o, log_sums, k, v, limit=60
    )
    kv = spread(kv).reshape(32, span, 2 * width)
    right = x_shift(mine, 1)
    left = x_shift(mine, -1)
    across = x_shift(mine, 2)

    i16 = jnp.arange(16, dtype=jnp.int32)
    bits = {axis: (i16 >> (3 - n)) & 1 for n, axis in enumerate(KV_AXES)}
    kv_ids = rank(bits["zh"], bits["zl"], xl, c, bits["yh"], bits["yl"], xh)
    q_ids = []
    for near_shifts, far_shifts in (((0,), (0,)), ((3, 1, 2), ()), ((), (3, 1, 2))):
        chosen = [(c, shift) for shift in near_shifts] + [(1 - c, shift) for shift in far_shifts]
        for cc, shift in chosen:
            xx = (x + shift) & 3
            q_ids.append(rank(zh, zl, xx & 1, cc, yh, yl, xx >> 1))
    ids = jnp.concatenate([kv_ids, jnp.stack(q_ids)])
    ids = (ids[:, None] * 2 + jnp.arange(2, dtype=jnp.int32)[None, :]).reshape(48)
    pos = lookup(span_order, ids)
    kv_pos, q_pos = pos[:32], pos[32:]
    place = jnp.sum((kv_pos[None, :] < kv_pos[:, None]).astype(jnp.int32), axis=1)
    hit = place[:, None] == jnp.arange(32, dtype=jnp.int32)[None, :]
    order = jnp.sum(jnp.where(hit, jnp.arange(32, dtype=jnp.int32)[:, None], 0), axis=0)
    sorted_pos = jnp.sum(jnp.where(hit, kv_pos[:, None], 0), axis=0)
    below = jnp.sum((kv_pos[None, :] < q_pos[:, None]).astype(jnp.int32), axis=1)
    own = jnp.sum((kv_pos[None, :] == q_pos[:, None]).astype(jnp.int32), axis=1)

    def tables(start, count):
        at = slice(start, start + count)
        return (order, sorted_pos, q_pos[at], below[at], own[at])

    first = (mine, swap(mine))
    dq, dq_far, *state = attend(tables(0, 4), (kv,), first, 2, True, False)
    near = (right, left, across)
    far = (swap(right), swap(left), swap(across))
    dq_near, dk, dv = attend(tables(4, 6), state, near, 6, False, False)
    state = (*state[:3], dk, dv)
    dq_back, dkv = attend(tables(10, 6), state, far, 0, False, True)
    dq_own = swap(dq_far)
    out = (dq_near + swap(dq_back).astype(f32)).astype(bf16)

    dkv = spread(dkv.reshape(16, tokens, 2 * width))
    shape = jax.ShapeDtypeStruct((tokens, width), bf16)
    dk, dv = local_call(functools.partial(finish_kernel, scale), (shape, shape), dkv)
    parts = [x_shift(out[:2], -1), x_shift(out[2:4], 1), x_shift(out[4:], 2)]
    shape = jax.ShapeDtypeStruct((heads, tokens, width), bf16)
    finish_dq = functools.partial(finish_dq_kernel, scale)
    return local_call(finish_dq, shape, dq, dq_own, *parts), dk, dv


def solution(mesh):
    fine = Mesh(mesh.devices.reshape((2,) * 7), AXES)
    return jax.shard_map(
        body,
        mesh=fine,
        in_specs=(
            P(None, AXES, None),
            P(AXES, None),
            P(AXES, None),
            P(None, AXES, None),
            P(None, AXES, None),
            P(None, AXES),
            P(),
        ),
        out_specs=(P(None, AXES, None), P(AXES, None), P(AXES, None)),
        check_vma=False,
    )
```

```python
import functools
import math

import jax
import jax.numpy as jnp
from jax import lax
from jax.experimental import pallas as pl
from jax.experimental.pallas import tpu as pltpu
from jax.sharding import Mesh
from jax.sharding import PartitionSpec as P


f32 = jnp.float32
bf16 = jnp.bfloat16
NT = (((1,), (1,)), ((), ()))
NN = (((1,), (0,)), ((), ()))
LOG2E = 1.0 / math.log(2.0)
AXES = ("zh", "zl", "xl", "c", "yh", "yl", "xh")
KV_AXES = ("zl", "yl", "zh", "yh")
WIDE = 4
UNROLLS = (4, 2, 1)
LIMIT = 24
STAT_ROWS = 32


def dot(a, b, dims):
    return lax.dot_general(a, b, dims, preferred_element_type=f32)


def kernel(first, last, counts, near, scale, order, sorted_pos, query_block, below, own, *rest):
    if first:
        kv_ref, rest = rest[0], rest[1:]
    else:
        (ks, vs, kt, dk_ref, dv_ref), rest = rest[:5], rest[5:]
    payloads, rest = rest[: len(counts)], rest[len(counts) :]
    near_ref = far_ref = None
    if near:
        near_ref, rest = rest[0], rest[1:]
    if near < sum(counts):
        far_ref, rest = rest[0], rest[1:]
    if first:
        (ks, vs, kt), rest = rest[:3], rest[3:]
    if last:
        dkv_ref, rest = rest[0], rest[1:]
    dk, dv, qd, st, dq = rest
    groups, _, width = qd.shape
    rows = st.shape[2]
    blocks = order.shape[0]
    span = ks.shape[0] // blocks
    chunk = WIDE * span
    if first:
        for r in range(blocks):
            block = kv_ref[order[r]]
            ks[r * span : (r + 1) * span, :] = block[:, :width]
            vs[r * span : (r + 1) * span, :] = block[:, width:]
        for r in range(0, blocks * span, chunk):
            kt[:, r : r + chunk] = ks[r : r + chunk, :].T
        dk[...] = jnp.zeros_like(dk)
        dv[...] = jnp.zeros_like(dv)
    else:
        dk[...] = dk_ref[...]
        dv[...] = dv_ref[...]
    lines = rows // width
    g = 0
    for ref, count in zip(payloads, counts):
        for i in range(count):
            qd[g] = ref[i, : 2 * rows, :]
            terms = ref[i, 2 * rows :, :].astype(f32)
            for kind in range(2):
                t = terms[kind * 3 * lines :]
                t = t[:lines] + t[lines : 2 * lines] + t[2 * lines : 3 * lines]
                st[g, kind : kind + 1, :] = jnp.concatenate(
                    [t[j : j + 1] for j in range(lines)], axis=1
                )
            g += 1

    def unit(g, first, count, size, masked):
        q, do = qd[g, :rows, :], qd[g, rows : 2 * rows, :]
        log_norm, delta = st[g, 0:1, :], st[g, 1:2, :]
        total = None
        for n in range(count):
            at = pl.ds(pl.multiple_of((first + n) * chunk, chunk), size * span)
            k, v = ks[at, :], vs[at, :]
            s = dot(k, q, NT)
            dp = dot(v, do, NT)
            p = jnp.exp2(s * (scale * LOG2E) - log_norm)
            if masked:
                lead = lax.rem(lax.broadcasted_iota(jnp.int32, (span, rows), 1), span)
                lead = lead - lax.broadcasted_iota(jnp.int32, (span, rows), 0)
                seen = [
                    lead + (query_block[g] - sorted_pos[(first + n) * WIDE + j]) * span
                    for j in range(size)
                ]
                p = jnp.where(jnp.concatenate(seen, axis=0) >= 0, p, 0.0)
            ds = (p * (dp - delta)).astype(bf16)
            dv[at, :] += dot(p.astype(bf16), do, NN)
            dk[at, :] += dot(ds, q, NN)
            part = dot(kt[:, at], ds, NN)
            total = part if total is None else total + part
        dq[...] += total

    def group(g, carry):
        dq[...] = jnp.zeros_like(dq)
        whole = below[g] // WIDE
        done = 0
        for count in UNROLLS:
            start = done
            turns = (whole - start) // count

            def step(i, carry, start=start, count=count):
                unit(g, start + i * count, count, WIDE, False)
                return carry

            lax.fori_loop(0, turns, step, 0)
            done = start + turns * count
        rest = below[g] + own[g] - whole * WIDE

        @pl.when((rest > 0) & (rest <= WIDE // 2))
        def _():
            unit(g, whole, 1, WIDE // 2, True)

        @pl.when(rest > WIDE // 2)
        def _():
            unit(g, whole, 1, WIDE, True)

        def store_near():
            for j in range(0, rows, width):
                near_ref[g, j : j + width, :] = dq[:, j : j + width].T

        def store_far():
            for j in range(0, rows, width):
                far_ref[g - near, j : j + width, :] = dq[:, j : j + width].T.astype(bf16)

        if far_ref is None:
            store_near()
        elif near_ref is None:
            store_far()
        else:
            pl.when(g < near)(store_near)
            pl.when(g >= near)(store_far)
        return carry

    lax.fori_loop(0, groups, group, 0)
    if last:
        for r in range(blocks):
            at = pl.ds(r * span, span)
            dkv_ref[order[r]] = jnp.concatenate([dk[at, :], dv[at, :]], axis=1).astype(
                dkv_ref.dtype
            )


def attend(tables, state, payloads, near, first, last):
    counts = tuple(p.shape[0] for p in payloads)
    groups = sum(counts)
    width = payloads[0].shape[2]
    rows = (payloads[0].shape[1] - STAT_ROWS) // 2
    blocks = tables[0].shape[0]
    if first:
        (kv,) = state
        keys = blocks * kv.shape[1]
    else:
        keys = state[0].shape[0]
    span = keys // blocks
    vmem = pl.BlockSpec(memory_space=pltpu.VMEM)
    smem = pl.BlockSpec(memory_space=pltpu.SMEM)
    scale = 1.0 / math.sqrt(width)
    pairs = groups * rows * keys // 2
    totals = [jax.ShapeDtypeStruct((keys, width), f32)] * 2
    out_shape = []
    if near:
        out_shape.append(jax.ShapeDtypeStruct((near, rows, width), f32))
    if near < groups:
        out_shape.append(jax.ShapeDtypeStruct((groups - near, rows, width), bf16))
    scratch = [
        pltpu.VMEM((groups, 2 * rows, width), bf16),
        pltpu.VMEM((groups, 2, rows), f32),
        pltpu.VMEM((width, rows), f32),
    ]
    if first:
        out_shape += [
            jax.ShapeDtypeStruct((keys, width), bf16),
            jax.ShapeDtypeStruct((keys, width), bf16),
            jax.ShapeDtypeStruct((width, keys), bf16),
        ]
    if last:
        out_shape.append(jax.ShapeDtypeStruct((blocks, span, 2 * width), bf16))
        scratch = [pltpu.VMEM((keys, width), f32)] * 2 + scratch
    else:
        out_shape += totals
    out_specs = [vmem] * len(out_shape)
    return pl.pallas_call(
        functools.partial(kernel, first, last, counts, near, scale),
        out_shape=tuple(out_shape),
        in_specs=[smem] * len(tables) + [vmem] * (len(state) + len(payloads)),
        out_specs=tuple(out_specs),
        scratch_shapes=scratch,
        cost_estimate=pl.CostEstimate(
            flops=pairs * width * 20, transcendentals=pairs, bytes_accessed=8 << 20
        ),
        compiler_params=pltpu.CompilerParams(vmem_limit_bytes=LIMIT << 20),
    )(*tables, *state, *payloads)


def prepare_kernel(q_ref, do_ref, o_ref, log_ref, k_ref, v_ref, mine_ref, kv_ref):
    heads, tokens, width = q_ref.shape
    span = tokens // 2
    rows = heads * span
    for j in range(kv_ref.shape[0]):
        kv_ref[j, :, :width] = k_ref[...]
        kv_ref[j, :, width:] = v_ref[...]
    ones = jnp.ones((8, width), bf16)
    log_norm = log_ref[...] * LOG2E
    turned = pltpu.roll(log_norm, span, 1)
    lower = lax.broadcasted_iota(jnp.int32, (1, tokens), 1) < span

    def terms(x):
        high = x.astype(bf16)
        rest = x - high.astype(f32)
        middle = rest.astype(bf16)
        low = (rest - middle.astype(f32)).astype(bf16)
        return [high.astype(f32), middle.astype(f32), low.astype(f32)]

    for s in range(2):
        at = slice(s * span, (s + 1) * span)
        mine_ref[s, :rows, :] = q_ref[:, at, :].reshape(rows, width)
        do = do_ref[:, at, :].reshape(rows, width)
        mine_ref[s, rows : 2 * rows, :] = do
        both = do.astype(f32) * o_ref[:, at, :].reshape(rows, width).astype(f32)
        high = both.astype(bf16)
        low = (both - high.astype(f32)).astype(bf16)
        delta = dot(ones, high, NT) + dot(ones, low, NT)
        delta = jnp.concatenate(
            [delta[0:1, j : j + width] for j in range(0, rows, width)], axis=0
        )
        first, second = (log_norm, turned) if s == 0 else (turned, log_norm)
        norms = jnp.concatenate(
            [
                jnp.where(lower, first[j : j + 1], second[j + 1 : j + 2])
                for j in range(0, heads, 2)
            ],
            axis=0,
        )
        pieces = terms(norms) + terms(delta)
        filled = sum(p.shape[0] for p in pieces)
        pieces.append(jnp.zeros((STAT_ROWS - filled, width), f32))
        mine_ref[s, 2 * rows :, :] = jnp.concatenate(pieces, axis=0).astype(bf16)


def local_call(function, out_shape, *args, limit=8):
    vmem = pl.BlockSpec(memory_space=pltpu.VMEM)
    many = isinstance(out_shape, tuple)
    return pl.pallas_call(
        function,
        out_shape=out_shape,
        in_specs=[vmem] * len(args),
        out_specs=(vmem,) * len(out_shape) if many else vmem,
        compiler_params=pltpu.CompilerParams(vmem_limit_bytes=limit << 20),
    )(*args)


def finish_kernel(scale, parts_ref, dk_ref, dv_ref):
    width = dk_ref.shape[1]
    total = parts_ref[0].astype(f32)
    for j in range(1, parts_ref.shape[0]):
        total = total + parts_ref[j].astype(f32)
    dk_ref[...] = (total[:, :width] * scale).astype(bf16)
    dv_ref[...] = total[:, width:].astype(bf16)


def finish_dq_kernel(scale, own_ref, *rest):
    parts, dq_ref = rest[:-1], rest[-1]
    heads, tokens, width = dq_ref.shape
    span = tokens // 2
    for s in range(2):
        total = own_ref[s]
        for ref in parts:
            total = total + ref[s].astype(f32)
        total = (total * scale).astype(bf16)
        dq_ref[:, s * span : (s + 1) * span, :] = total.reshape(heads, span, width)


def lookup(table, ids):
    hits = ids[:, None] == jnp.arange(table.shape[0], dtype=jnp.int32)[None, :]
    return jnp.sum(jnp.where(hits, table[None, :], 0), axis=1)


def rank(zh, zl, xl, c, yh, yl, xh):
    out = 0
    for bit in (zh, zl, xl, c, yh, yl, xh):
        out = out * 2 + bit
    return out


def x_shift(a, by):
    at = lambda x: (x % 2) * 2 + x // 2
    return lax.ppermute(a, ("xl", "xh"), [(at(x), at((x + by) % 4)) for x in range(4)])


def swap(a):
    return lax.ppermute(a, "c", [(0, 1), (1, 0)])


def spread(a):
    return lax.all_to_all(a, KV_AXES, 0, 0, tiled=True)


def body(q, k, v, o, do, log_sums, span_order):
    heads, tokens, width = q.shape
    span = tokens // 2
    scale = 1.0 / math.sqrt(width)
    zh, zl, xl, c, yh, yl, xh = [lax.axis_index(a) for a in AXES]
    x = xh * 2 + xl

    payload = jax.ShapeDtypeStruct((2, heads * tokens + STAT_ROWS, width), bf16)
    copies = jax.ShapeDtypeStruct((16, tokens, 2 * width), bf16)
    mine, kv = local_call(
        prepare_kernel, (payload, copies), q, do, o, log_sums, k, v, limit=60
    )
    kv = spread(kv).reshape(32, span, 2 * width)
    right = x_shift(mine, 1)
    left = x_shift(mine, -1)
    across = x_shift(mine, 2)

    i16 = jnp.arange(16, dtype=jnp.int32)
    bits = {axis: (i16 >> (3 - n)) & 1 for n, axis in enumerate(KV_AXES)}
    kv_ids = rank(bits["zh"], bits["zl"], xl, c, bits["yh"], bits["yl"], xh)
    q_ids = []
    for near_shifts, far_shifts in (((0,), (0,)), ((3, 1, 2), ()), ((), (3, 1, 2))):
        chosen = [(c, shift) for shift in near_shifts] + [(1 - c, shift) for shift in far_shifts]
        for cc, shift in chosen:
            xx = (x + shift) & 3
            q_ids.append(rank(zh, zl, xx & 1, cc, yh, yl, xx >> 1))
    ids = jnp.concatenate([kv_ids, jnp.stack(q_ids)])
    ids = (ids[:, None] * 2 + jnp.arange(2, dtype=jnp.int32)[None, :]).reshape(48)
    pos = lookup(span_order, ids)
    kv_pos, q_pos = pos[:32], pos[32:]
    place = jnp.sum((kv_pos[None, :] < kv_pos[:, None]).astype(jnp.int32), axis=1)
    hit = place[:, None] == jnp.arange(32, dtype=jnp.int32)[None, :]
    order = jnp.sum(jnp.where(hit, jnp.arange(32, dtype=jnp.int32)[:, None], 0), axis=0)
    sorted_pos = jnp.sum(jnp.where(hit, kv_pos[:, None], 0), axis=0)
    below = jnp.sum((kv_pos[None, :] < q_pos[:, None]).astype(jnp.int32), axis=1)
    own = jnp.sum((kv_pos[None, :] == q_pos[:, None]).astype(jnp.int32), axis=1)

    def tables(start, count):
        at = slice(start, start + count)
        return (order, sorted_pos, q_pos[at], below[at], own[at])

    first = (mine, swap(mine))
    dq, dq_far, *state = attend(tables(0, 4), (kv,), first, 2, True, False)
    near = (right, left, across)
    far = (swap(right), swap(left), swap(across))
    dq_near, dk, dv = attend(tables(4, 6), state, near, 6, False, False)
    state = (*state[:3], dk, dv)
    dq_back, dkv = attend(tables(10, 6), state, far, 0, False, True)
    dq_own = swap(dq_far)
    out = (dq_near + swap(dq_back).astype(f32)).astype(bf16)

    dkv = spread(dkv.reshape(16, tokens, 2 * width))
    shape = jax.ShapeDtypeStruct((tokens, width), bf16)
    dk, dv = local_call(functools.partial(finish_kernel, scale), (shape, shape), dkv)
    parts = [x_shift(out[:2], -1), x_shift(out[2:4], 1), x_shift(out[4:], 2)]
    shape = jax.ShapeDtypeStruct((heads, tokens, width), bf16)
    finish_dq = functools.partial(finish_dq_kernel, scale)
    return local_call(finish_dq, shape, dq, dq_own, *parts), dk, dv


def solution(mesh):
    fine = Mesh(mesh.devices.reshape((2,) * 7), AXES)
    return jax.shard_map(
        body,
        mesh=fine,
        in_specs=(
            P(None, AXES, None),
            P(AXES, None),
            P(AXES, None),
            P(None, AXES, None),
            P(None, AXES, None),
            P(None, AXES),
            P(),
        ),
        out_specs=(P(None, AXES, None), P(AXES, None), P(AXES, None)),
        check_vma=False,
    )
```

```python
import functools
import math

import jax
import jax.numpy as jnp
from jax import lax
from jax.experimental import pallas as pl
from jax.experimental.pallas import tpu as pltpu
from jax.sharding import Mesh
from jax.sharding import PartitionSpec as P


f32 = jnp.float32
bf16 = jnp.bfloat16
NT = (((1,), (1,)), ((), ()))
NN = (((1,), (0,)), ((), ()))
LOG2E = 1.0 / math.log(2.0)
AXES = ("zh", "zl", "xl", "c", "yh", "yl", "xh")
KV_AXES = ("zl", "yl", "zh", "yh")
WIDE = 4
UNROLLS = (4, 3, 2, 1)
LIMIT = 24
STAT_ROWS = 32


def dot(a, b, dims):
    return lax.dot_general(a, b, dims, preferred_element_type=f32)


def kernel(first, last, counts, near, scale, order, sorted_pos, query_block, below, own, *rest):
    if first:
        kv_ref, rest = rest[0], rest[1:]
    else:
        (ks, vs, kt, dk_ref, dv_ref), rest = rest[:5], rest[5:]
    payloads, rest = rest[: len(counts)], rest[len(counts) :]
    near_ref = far_ref = None
    if near:
        near_ref, rest = rest[0], rest[1:]
    if near < sum(counts):
        far_ref, rest = rest[0], rest[1:]
    if first:
        (ks, vs, kt), rest = rest[:3], rest[3:]
    if last:
        dkv_ref, rest = rest[0], rest[1:]
    dk, dv, qd, st, dq = rest
    groups, _, width = qd.shape
    rows = st.shape[2]
    blocks = order.shape[0]
    span = ks.shape[0] // blocks
    chunk = WIDE * span
    if first:
        for r in range(blocks):
            block = kv_ref[order[r]]
            ks[r * span : (r + 1) * span, :] = block[:, :width]
            vs[r * span : (r + 1) * span, :] = block[:, width:]
        for r in range(0, blocks * span, chunk):
            kt[:, r : r + chunk] = ks[r : r + chunk, :].T
        dk[...] = jnp.zeros_like(dk)
        dv[...] = jnp.zeros_like(dv)
    else:
        dk[...] = dk_ref[...]
        dv[...] = dv_ref[...]
    lines = rows // width
    g = 0
    for ref, count in zip(payloads, counts):
        for i in range(count):
            qd[g] = ref[i, : 2 * rows, :]
            terms = ref[i, 2 * rows :, :].astype(f32)
            for kind in range(2):
                t = terms[kind * 3 * lines :]
                t = t[:lines] + t[lines : 2 * lines] + t[2 * lines : 3 * lines]
                st[g, kind : kind + 1, :] = jnp.concatenate(
                    [t[j : j + 1] for j in range(lines)], axis=1
                )
            g += 1

    def unit(g, first, count, size, masked):
        q, do = qd[g, :rows, :], qd[g, rows : 2 * rows, :]
        log_norm, delta = st[g, 0:1, :], st[g, 1:2, :]
        total = None
        for n in range(count):
            at = pl.ds(pl.multiple_of((first + n) * chunk, chunk), size * span)
            k, v = ks[at, :], vs[at, :]
            s = dot(k, q, NT)
            dp = dot(v, do, NT)
            p = jnp.exp2(s * (scale * LOG2E) - log_norm)
            if masked:
                lead = lax.rem(lax.broadcasted_iota(jnp.int32, (span, rows), 1), span)
                lead = lead - lax.broadcasted_iota(jnp.int32, (span, rows), 0)
                seen = [
                    lead + (query_block[g] - sorted_pos[(first + n) * WIDE + j]) * span
                    for j in range(size)
                ]
                p = jnp.where(jnp.concatenate(seen, axis=0) >= 0, p, 0.0)
            ds = (p * (dp - delta)).astype(bf16)
            dv[at, :] += dot(p.astype(bf16), do, NN)
            dk[at, :] += dot(ds, q, NN)
            part = dot(kt[:, at], ds, NN)
            total = part if total is None else total + part
        dq[...] += total

    def group(g, carry):
        dq[...] = jnp.zeros_like(dq)
        whole = below[g] // WIDE
        done = 0
        for count in UNROLLS:
            start = done
            turns = (whole - start) // count

            def step(i, carry, start=start, count=count):
                unit(g, start + i * count, count, WIDE, False)
                return carry

            lax.fori_loop(0, turns, step, 0)
            done = start + turns * count
        rest = below[g] + own[g] - whole * WIDE

        for size in range(1, WIDE + 1):

            @pl.when(rest == size)
            def _(size=size):
                unit(g, whole, 1, size, True)

        def store_near():
            for j in range(0, rows, width):
                near_ref[g, j : j + width, :] = dq[:, j : j + width].T

        def store_far():
            for j in range(0, rows, width):
                far_ref[g - near, j : j + width, :] = dq[:, j : j + width].T.astype(bf16)

        if far_ref is None:
            store_near()
        elif near_ref is None:
            store_far()
        else:
            pl.when(g < near)(store_near)
            pl.when(g >= near)(store_far)
        return carry

    lax.fori_loop(0, groups, group, 0)
    if last:
        for r in range(blocks):
            at = pl.ds(r * span, span)
            dkv_ref[order[r]] = jnp.concatenate([dk[at, :], dv[at, :]], axis=1).astype(
                dkv_ref.dtype
            )


def attend(tables, state, payloads, near, first, last):
    counts = tuple(p.shape[0] for p in payloads)
    groups = sum(counts)
    width = payloads[0].shape[2]
    rows = (payloads[0].shape[1] - STAT_ROWS) // 2
    blocks = tables[0].shape[0]
    if first:
        (kv,) = state
        keys = blocks * kv.shape[1]
    else:
        keys = state[0].shape[0]
    span = keys // blocks
    vmem = pl.BlockSpec(memory_space=pltpu.VMEM)
    smem = pl.BlockSpec(memory_space=pltpu.SMEM)
    scale = 1.0 / math.sqrt(width)
    pairs = groups * rows * keys // 2
    totals = [jax.ShapeDtypeStruct((keys, width), f32)] * 2
    out_shape = []
    if near:
        out_shape.append(jax.ShapeDtypeStruct((near, rows, width), f32))
    if near < groups:
        out_shape.append(jax.ShapeDtypeStruct((groups - near, rows, width), bf16))
    scratch = [
        pltpu.VMEM((groups, 2 * rows, width), bf16),
        pltpu.VMEM((groups, 2, rows), f32),
        pltpu.VMEM((width, rows), f32),
    ]
    if first:
        out_shape += [
            jax.ShapeDtypeStruct((keys, width), bf16),
            jax.ShapeDtypeStruct((keys, width), bf16),
            jax.ShapeDtypeStruct((width, keys), bf16),
        ]
    if last:
        out_shape.append(jax.ShapeDtypeStruct((blocks, span, 2 * width), bf16))
        scratch = [pltpu.VMEM((keys, width), f32)] * 2 + scratch
    else:
        out_shape += totals
    out_specs = [vmem] * len(out_shape)
    return pl.pallas_call(
        functools.partial(kernel, first, last, counts, near, scale),
        out_shape=tuple(out_shape),
        in_specs=[smem] * len(tables) + [vmem] * (len(state) + len(payloads)),
        out_specs=tuple(out_specs),
        scratch_shapes=scratch,
        cost_estimate=pl.CostEstimate(
            flops=pairs * width * 20, transcendentals=pairs, bytes_accessed=8 << 20
        ),
        compiler_params=pltpu.CompilerParams(vmem_limit_bytes=LIMIT << 20),
    )(*tables, *state, *payloads)


def prepare_kernel(q_ref, do_ref, o_ref, log_ref, k_ref, v_ref, mine_ref, kv_ref):
    heads, tokens, width = q_ref.shape
    span = tokens // 2
    rows = heads * span
    for j in range(kv_ref.shape[0]):
        kv_ref[j, :, :width] = k_ref[...]
        kv_ref[j, :, width:] = v_ref[...]
    ones = jnp.ones((8, width), bf16)
    log_norm = log_ref[...] * LOG2E
    turned = pltpu.roll(log_norm, span, 1)
    lower = lax.broadcasted_iota(jnp.int32, (1, tokens), 1) < span

    def terms(x):
        high = x.astype(bf16)
        rest = x - high.astype(f32)
        middle = rest.astype(bf16)
        low = (rest - middle.astype(f32)).astype(bf16)
        return [high.astype(f32), middle.astype(f32), low.astype(f32)]

    for s in range(2):
        at = slice(s * span, (s + 1) * span)
        mine_ref[s, :rows, :] = q_ref[:, at, :].reshape(rows, width)
        do = do_ref[:, at, :].reshape(rows, width)
        mine_ref[s, rows : 2 * rows, :] = do
        both = do.astype(f32) * o_ref[:, at, :].reshape(rows, width).astype(f32)
        high = both.astype(bf16)
        low = (both - high.astype(f32)).astype(bf16)
        delta = dot(ones, high, NT) + dot(ones, low, NT)
        delta = jnp.concatenate(
            [delta[0:1, j : j + width] for j in range(0, rows, width)], axis=0
        )
        first, second = (log_norm, turned) if s == 0 else (turned, log_norm)
        norms = jnp.concatenate(
            [
                jnp.where(lower, first[j : j + 1], second[j + 1 : j + 2])
                for j in range(0, heads, 2)
            ],
            axis=0,
        )
        pieces = terms(norms) + terms(delta)
        filled = sum(p.shape[0] for p in pieces)
        pieces.append(jnp.zeros((STAT_ROWS - filled, width), f32))
        mine_ref[s, 2 * rows :, :] = jnp.concatenate(pieces, axis=0).astype(bf16)


def local_call(function, out_shape, *args, limit=8):
    vmem = pl.BlockSpec(memory_space=pltpu.VMEM)
    many = isinstance(out_shape, tuple)
    return pl.pallas_call(
        function,
        out_shape=out_shape,
        in_specs=[vmem] * len(args),
        out_specs=(vmem,) * len(out_shape) if many else vmem,
        compiler_params=pltpu.CompilerParams(vmem_limit_bytes=limit << 20),
    )(*args)


def finish_kernel(scale, parts_ref, dk_ref, dv_ref):
    width = dk_ref.shape[1]
    total = parts_ref[0].astype(f32)
    for j in range(1, parts_ref.shape[0]):
        total = total + parts_ref[j].astype(f32)
    dk_ref[...] = (total[:, :width] * scale).astype(bf16)
    dv_ref[...] = total[:, width:].astype(bf16)


def finish_dq_kernel(scale, own_ref, *rest):
    parts, dq_ref = rest[:-1], rest[-1]
    heads, tokens, width = dq_ref.shape
    span = tokens // 2
    for s in range(2):
        total = own_ref[s]
        for ref in parts:
            total = total + ref[s].astype(f32)
        total = (total * scale).astype(bf16)
        dq_ref[:, s * span : (s + 1) * span, :] = total.reshape(heads, span, width)


def lookup(table, ids):
    hits = ids[:, None] == jnp.arange(table.shape[0], dtype=jnp.int32)[None, :]
    return jnp.sum(jnp.where(hits, table[None, :], 0), axis=1)


def rank(zh, zl, xl, c, yh, yl, xh):
    out = 0
    for bit in (zh, zl, xl, c, yh, yl, xh):
        out = out * 2 + bit
    return out


def x_shift(a, by):
    at = lambda x: (x % 2) * 2 + x // 2
    return lax.ppermute(a, ("xl", "xh"), [(at(x), at((x + by) % 4)) for x in range(4)])


def swap(a):
    return lax.ppermute(a, "c", [(0, 1), (1, 0)])


def spread(a):
    return lax.all_to_all(a, KV_AXES, 0, 0, tiled=True)


def body(q, k, v, o, do, log_sums, span_order):
    heads, tokens, width = q.shape
    span = tokens // 2
    scale = 1.0 / math.sqrt(width)
    zh, zl, xl, c, yh, yl, xh = [lax.axis_index(a) for a in AXES]
    x = xh * 2 + xl

    payload = jax.ShapeDtypeStruct((2, heads * tokens + STAT_ROWS, width), bf16)
    copies = jax.ShapeDtypeStruct((16, tokens, 2 * width), bf16)
    mine, kv = local_call(
        prepare_kernel, (payload, copies), q, do, o, log_sums, k, v, limit=60
    )
    kv = spread(kv).reshape(32, span, 2 * width)
    right = x_shift(mine, 1)
    left = x_shift(mine, -1)
    across = x_shift(mine, 2)

    i16 = jnp.arange(16, dtype=jnp.int32)
    bits = {axis: (i16 >> (3 - n)) & 1 for n, axis in enumerate(KV_AXES)}
    kv_ids = rank(bits["zh"], bits["zl"], xl, c, bits["yh"], bits["yl"], xh)
    q_ids = []
    for near_shifts, far_shifts in (((0,), (0,)), ((3, 1, 2), ()), ((), (3, 1, 2))):
        chosen = [(c, shift) for shift in near_shifts] + [(1 - c, shift) for shift in far_shifts]
        for cc, shift in chosen:
            xx = (x + shift) & 3
            q_ids.append(rank(zh, zl, xx & 1, cc, yh, yl, xx >> 1))
    ids = jnp.concatenate([kv_ids, jnp.stack(q_ids)])
    ids = (ids[:, None] * 2 + jnp.arange(2, dtype=jnp.int32)[None, :]).reshape(48)
    pos = lookup(span_order, ids)
    kv_pos, q_pos = pos[:32], pos[32:]
    place = jnp.sum((kv_pos[None, :] < kv_pos[:, None]).astype(jnp.int32), axis=1)
    hit = place[:, None] == jnp.arange(32, dtype=jnp.int32)[None, :]
    order = jnp.sum(jnp.where(hit, jnp.arange(32, dtype=jnp.int32)[:, None], 0), axis=0)
    sorted_pos = jnp.sum(jnp.where(hit, kv_pos[:, None], 0), axis=0)
    below = jnp.sum((kv_pos[None, :] < q_pos[:, None]).astype(jnp.int32), axis=1)
    own = jnp.sum((kv_pos[None, :] == q_pos[:, None]).astype(jnp.int32), axis=1)

    def tables(start, count):
        at = slice(start, start + count)
        return (order, sorted_pos, q_pos[at], below[at], own[at])

    first = (mine, swap(mine))
    dq, dq_far, *state = attend(tables(0, 4), (kv,), first, 2, True, False)
    near = (right, left, across)
    far = (swap(right), swap(left), swap(across))
    dq_near, dk, dv = attend(tables(4, 6), state, near, 6, False, False)
    state = (*state[:3], dk, dv)
    dq_back, dkv = attend(tables(10, 6), state, far, 0, False, True)
    dq_own = swap(dq_far)
    out = (dq_near + swap(dq_back).astype(f32)).astype(bf16)

    dkv = spread(dkv.reshape(16, tokens, 2 * width))
    shape = jax.ShapeDtypeStruct((tokens, width), bf16)
    dk, dv = local_call(functools.partial(finish_kernel, scale), (shape, shape), dkv)
    parts = [x_shift(out[:2], -1), x_shift(out[2:4], 1), x_shift(out[4:], 2)]
    shape = jax.ShapeDtypeStruct((heads, tokens, width), bf16)
    finish_dq = functools.partial(finish_dq_kernel, scale)
    return local_call(finish_dq, shape, dq, dq_own, *parts), dk, dv


def solution(mesh):
    fine = Mesh(mesh.devices.reshape((2,) * 7), AXES)
    return jax.shard_map(
        body,
        mesh=fine,
        in_specs=(
            P(None, AXES, None),
            P(AXES, None),
            P(AXES, None),
            P(None, AXES, None),
            P(None, AXES, None),
            P(None, AXES),
            P(),
        ),
        out_specs=(P(None, AXES, None), P(AXES, None), P(AXES, None)),
        check_vma=False,
    )
```
